32 devices in a mesh: blk: 8 (over z, core), pair: 2 (over x), head: 2 (over y).
Axes of the slice: x: 2, y: 2, z: 4, core: 2. Of those that a mesh axis runs over, the one named last changes fastest.
Arguments:
- prefix_query_rows: bfloat16 [1024, 8, 8, 128], P('blk', 'head', 'pair'), may hold values from -6 to 6
- prefix_key_rows: bfloat16 [1024, 8, 128], P('blk', 'head'), may hold values from -6 to 6
- prefix_value_rows: bfloat16 [1024, 8, 128], P('blk', 'head'), may hold values from -6 to 6
- prefix_output_gradient: bfloat16 [1024, 8, 8, 128], P('blk', 'head', 'pair'), may hold values from -6 to 6
- resp_q: bfloat16 [2, 1024, 8, 8, 128], P('pair', 'blk', 'head'), may hold values from -100 to 100
- resp_k: bfloat16 [2, 1024, 8, 128], P('pair', 'blk', 'head'), may hold values from -4 to 4
- response_value_rows: bfloat16 [2, 1024, 8, 128], P('pair', 'blk', 'head'), may hold values from -6 to 6
- response_output_gradient: bfloat16 [2, 1024, 8, 8, 128], P('pair', 'blk', 'head'), may hold values from -6 to 6
- lengths: int32 [2], replicated, may hold values from 128 to 1024, as said below
- prefix_order: int32 [8], replicated, may hold values from 0 to 7, each once
Outputs:
- dprefix_q: bfloat16 [1024, 8, 8, 128], P(('blk', 'head'), None, 'pair')
- dprefix_k: bfloat16 [1024, 8, 128], P(('blk', 'head'))
- dprefix_v: bfloat16 [1024, 8, 128], P(('blk', 'head'))
- dresp_q: bfloat16 [2, 1024, 8, 8, 128], P('pair', ('blk', 'head'))
- dresp_k: bfloat16 [2, 1024, 8, 128], P('pair', ('blk', 'head'))
- dresp_v: bfloat16 [2, 1024, 8, 128], P('pair', ('blk', 'head'))
The draws below stay inside these ranges and needn't reach their ends.
Inputs may be any that keep to these rules, and one draw needn't show every extreme that they name: `prefix_order`: the stored prefix blocks are the prefix blocks 0 to 7, each once. Each length is a multiple of 128; one of the two lengths equals 1024.
All inputs are finite; a program needn't handle non-finite values.
Results may differ from the reference program's by a relative error of at most 0.0051.
Values may be sent and summed in bfloat16 or wider, within the bound.
No kernel may reach another device: no remote copies, remote signals or barrier semaphores. Data moves between devices by JAX's collectives and lax.ppermute only.
A program may use at most 192 MiB of HBM per device.

```python
import jax
import jax.numpy as jnp
from jax import lax

HEAD_DIM = 128
KEY_VALUE_HEADS = 8
QUERY_GROUP = 8
PBLK = 128
PREFIX_LENGTH = 1024
RESPONSE_LENGTH = 1024
NPB = 8


def random_key_table(key):
    base_random = jnp.clip(jax.random.normal(jax.random.fold_in(key, 101), (2, RESPONSE_LENGTH, KEY_VALUE_HEADS, HEAD_DIM), jnp.float32), -4.0, 4.0)
    return base_random


def draw_resp_k(key, part):
    return random_key_table(key).astype(jnp.bfloat16)


def draw_resp_q(key, part):
    return jnp.clip(jax.random.normal(jax.random.fold_in(key, 203), (2, RESPONSE_LENGTH, KEY_VALUE_HEADS, QUERY_GROUP, HEAD_DIM), jnp.float32), -4.0, 4.0).astype(jnp.bfloat16)


def draw_lengths(key, part):
    full_side = jax.random.randint(jax.random.fold_in(key, 301), (), 0, 2)
    other = jax.random.randint(jax.random.fold_in(key, 302), (), 1, RESPONSE_LENGTH // PBLK + 1) * PBLK
    return jnp.where(jnp.arange(2) == full_side, RESPONSE_LENGTH, other).astype(jnp.int32)


def levels(key, dims, shards, least, largest):
    def one(position, blocks):
        steps = jax.random.uniform(jax.random.fold_in(jax.random.fold_in(key, 6), position), (blocks,), jnp.float32, least / len(shards), largest / len(shards))
        return jnp.repeat(jnp.exp(steps), dims[position] // blocks).reshape((-1,) + (1,) * (len(dims) - position - 1))

    gain = one(*shards[0])
    for cut in shards[1:]:
        gain = gain * one(*cut)
    return gain


def gaussian(rng, extent, deviation, reach, split=(), kind=jnp.bfloat16):
    values = jax.random.normal(rng, extent, jnp.float32) * deviation
    if len(split) > 0:
        values = levels(rng, extent, split, -0.22, 0.18) * values
    return jnp.clip(values, min=-reach, max=reach).astype(kind)


def setup_inputs(seed: int = 0) -> dict:
    splits = jax.random.split(jax.random.key(seed), 11)
    return {
        "prefix_query_rows": gaussian(splits[0], (PREFIX_LENGTH, KEY_VALUE_HEADS, QUERY_GROUP, HEAD_DIM), 1.0, 6.0, ((0, 8), (1, 2), (2, 2))),
        "prefix_key_rows": gaussian(splits[1], (PREFIX_LENGTH, KEY_VALUE_HEADS, HEAD_DIM), 1.0, 6.0, ((0, 8), (1, 2))),
        "prefix_value_rows": gaussian(splits[2], (PREFIX_LENGTH, KEY_VALUE_HEADS, HEAD_DIM), 1.0, 6.0, ((0, 8), (1, 2))),
        "prefix_output_gradient": gaussian(splits[3], (PREFIX_LENGTH, KEY_VALUE_HEADS, QUERY_GROUP, HEAD_DIM), 1.0, 6.0, ((0, 8), (1, 2), (2, 2))),
        "resp_q": draw_resp_q(jax.random.fold_in(splits[10], 71), 0),
        "resp_k": draw_resp_k(jax.random.fold_in(splits[10], 71), 0),
        "response_value_rows": gaussian(splits[6], (2, RESPONSE_LENGTH, KEY_VALUE_HEADS, HEAD_DIM), 1.0, 6.0, ((0, 2), (1, 8), (2, 2))),
        "response_output_gradient": gaussian(splits[7], (2, RESPONSE_LENGTH, KEY_VALUE_HEADS, QUERY_GROUP, HEAD_DIM), 1.0, 6.0, ((0, 2), (1, 8), (2, 2))),
        "lengths": draw_lengths(jax.random.fold_in(splits[10], 71), 0),
        "prefix_order": jax.random.permutation(splits[9], NPB).astype(jnp.int32),
    }


very_low = -1e30


def attention_grads(queries, query_pos, grad_outs, random_keys, key_pos, values):
    scaling = HEAD_DIM ** -0.5
    logits = jnp.dot(queries, random_keys.T, preferred_element_type=jnp.float32) * scaling
    visible = key_pos[None, :] <= query_pos[:, None]
    peak = jnp.max(jnp.where(visible, logits, very_low), axis=1)
    expo = jnp.where(visible, jnp.exp(logits - peak[:, None]), 0.0)
    log_total = peak + jnp.log(jnp.sum(expo, axis=1))
    softmax = jnp.where(visible, jnp.exp(logits - log_total[:, None]), 0.0)
    dprobs = jnp.dot(grad_outs, values.T, preferred_element_type=jnp.float32)
    deltas = jnp.sum(softmax * dprobs, axis=1)
    dscores = (softmax * (dprobs - deltas[:, None]) * scaling).astype(jnp.bfloat16)
    soft_bf = softmax.astype(jnp.bfloat16)
    grad_q = jnp.dot(dscores, random_keys, preferred_element_type=jnp.float32)
    grad_k = jnp.dot(dscores.T, queries, preferred_element_type=jnp.float32)
    grad_v = jnp.dot(soft_bf.T, grad_outs, preferred_element_type=jnp.float32)
    return grad_q, grad_k, grad_v


def reference(prefix_query_rows, prefix_key_rows, prefix_value_rows, prefix_output_gradient, resp_q, resp_k, response_value_rows, response_output_gradient, lengths, prefix_order):
    prefix_pos = (prefix_order[:, None] * PBLK + jnp.arange(PBLK, dtype=jnp.int32)[None, :]).reshape(PREFIX_LENGTH).astype(jnp.int32)
    resp_pos = (PREFIX_LENGTH + jnp.arange(RESPONSE_LENGTH, dtype=jnp.int32)).astype(jnp.int32)
    key_pos = jnp.concatenate([prefix_pos, resp_pos]).astype(jnp.int32)
    live_rows = jnp.arange(RESPONSE_LENGTH, dtype=jnp.int32)[None, :] < lengths[:, None]
    live_dout = jnp.where(live_rows[:, :, None, None, None], response_output_gradient, jnp.zeros((), response_output_gradient.dtype))

    def per_head(items):
        head_q, head_k, head_v, head_do, rq, rk, rv, rdo = items
        grad_q, grad_k, grad_v = attention_grads(head_q.reshape(PREFIX_LENGTH * QUERY_GROUP, HEAD_DIM), jnp.repeat(prefix_pos, QUERY_GROUP), head_do.reshape(PREFIX_LENGTH * QUERY_GROUP, HEAD_DIM), head_k, prefix_pos, head_v)
        resp_dq = []
        resp_dk = []
        resp_dv = []
        for which_side in range(2):
            random_keys = jnp.concatenate([head_k, rk[which_side]], axis=0)
            values = jnp.concatenate([head_v, rv[which_side]], axis=0)
            part_q, part_k, part_v = attention_grads(rq[which_side].reshape(RESPONSE_LENGTH * QUERY_GROUP, HEAD_DIM), jnp.repeat(resp_pos, QUERY_GROUP), rdo[which_side].reshape(RESPONSE_LENGTH * QUERY_GROUP, HEAD_DIM), random_keys, key_pos, values)
            grad_k = grad_k + part_k[:PREFIX_LENGTH]
            grad_v = grad_v + part_v[:PREFIX_LENGTH]
            resp_dq.append(part_q.reshape(RESPONSE_LENGTH, QUERY_GROUP, HEAD_DIM).astype(jnp.bfloat16))
            resp_dk.append(part_k[PREFIX_LENGTH:].astype(jnp.bfloat16))
            resp_dv.append(part_v[PREFIX_LENGTH:].astype(jnp.bfloat16))
        return (grad_q.reshape(PREFIX_LENGTH, QUERY_GROUP, HEAD_DIM).astype(jnp.bfloat16), grad_k.astype(jnp.bfloat16), grad_v.astype(jnp.bfloat16), jnp.stack(resp_dq), jnp.stack(resp_dk), jnp.stack(resp_dv))

    items = (jnp.moveaxis(prefix_query_rows, 1, 0), jnp.moveaxis(prefix_key_rows, 1, 0), jnp.moveaxis(prefix_value_rows, 1, 0), jnp.moveaxis(prefix_output_gradient, 1, 0), jnp.moveaxis(resp_q, 2, 0), jnp.moveaxis(resp_k, 2, 0), jnp.moveaxis(response_value_rows, 2, 0), jnp.moveaxis(live_dout, 2, 0))
    grad_pq, grad_pk, grad_pv, grad_rq, grad_rk, grad_rv = lax.map(per_head, items)
    return (jnp.moveaxis(grad_pq, 0, 1), jnp.moveaxis(grad_pk, 0, 1), jnp.moveaxis(grad_pv, 0, 1), jnp.moveaxis(grad_rq, 0, 2), jnp.moveaxis(grad_rk, 0, 2), jnp.moveaxis(grad_rv, 0, 2))
```

```python
import functools
import math

import jax
import jax.numpy as jnp
from jax import lax
from jax.experimental import pallas as pl
from jax.experimental.pallas import tpu as pltpu
from jax.sharding import Mesh, PartitionSpec as P

F32 = jnp.float32
BF16 = jnp.bfloat16
very_low = -1e30


def dot_nt(a, b):
    return lax.dot_general(a, b, (((1,), (1,)), ((), ())), preferred_element_type=F32)


def dot_nn(a, b):
    return lax.dot_general(a, b, (((1,), (0,)), ((), ())), preferred_element_type=F32)


def dot_tn(a, b):
    return lax.dot_general(a, b, (((0,), (0,)), ((), ())), preferred_element_type=F32)


def attn_kernel(
    order,
    lengths,
    qp_ref,
    qr_ref,
    dop_ref,
    dor_ref,
    kv_ref,
    dq_ref,
    dkv_ref,
    q_sc,
    do_sc,
    k_sc,
    v_sc,
    dk_sc,
    dv_sc,
    e_sc,
    p_sc,
    m_sc,
    *,
    blocks,
    slots,
    rows,
    half,
    full,
    chunk,
    first_block,
    side,
):
    step = pl.program_id(1)
    tile = rows * half
    per_slot = 1 + full // half
    slot = step // per_slot
    part = step % per_slot
    head_size = qp_ref.shape[-1]
    scaling = head_size**-0.5
    cexp = scaling * math.log2(math.e)
    total = blocks * rows
    block = first_block() + slot

    @pl.when(step == 0)
    def _():
        for j in range(blocks):
            at = pl.multiple_of(order[j] * rows, rows)
            k_sc[pl.ds(at, rows), :] = kv_ref[j, 0, 0, :rows, :]
            v_sc[pl.ds(at, rows), :] = kv_ref[j, 1, 0, :rows, :]
            k_sc[pl.ds(total + j * rows, rows), :] = kv_ref[j, 0, 0, rows:, :]
            v_sc[pl.ds(total + j * rows, rows), :] = kv_ref[j, 1, 0, rows:, :]
        dk_sc[...] = jnp.zeros_like(dk_sc)
        dv_sc[...] = jnp.zeros_like(dv_sc)

    @pl.when(part == 0)
    def _():
        q_sc[...] = qp_ref[0, 0]
        do_sc[...] = dop_ref[0, 0]

    @pl.when(part > 0)
    def _():
        q_sc[...] = qr_ref[0, 0]
        do_sc[...] = dor_ref[0, 0]

    sub = tile // full
    pos0 = jnp.where(part == 0, order[block] * rows, total + block * rows + (part - 1) * sub)
    shift = jnp.where(part == 0, int(math.log2(half)), int(math.log2(full)))
    live = jnp.logical_or(part == 0, block * rows < lengths[side()])
    nfull = (pos0 + 1) // chunk

    def run():
        q = q_sc[...]
        do = do_sc[...]

        def scores(c, carry, masked):
            m, l, dl = carry
            base = pl.multiple_of(c * chunk, chunk)
            s = dot_nt(k_sc[pl.ds(base, chunk), :], q) * cexp
            if masked:
                kp = base + lax.broadcasted_iota(jnp.int32, (chunk, tile), 0)
                qp = pos0 + lax.shift_right_logical(
                    lax.broadcasted_iota(jnp.int32, (chunk, tile), 1), shift
                )
                s = jnp.where(kp <= qp, s, very_low)
            new = jnp.maximum(m, jnp.max(s, axis=0, keepdims=True))
            e = jnp.exp2(s - new)
            dp = dot_nt(v_sc[pl.ds(base, chunk), :], do)
            a = jnp.exp2(m - new)
            l = l * a + jnp.sum(e, axis=0, keepdims=True)
            dl = dl * a + jnp.sum(e * dp, axis=0, keepdims=True)
            e_sc[pl.ds(base, chunk), :] = e
            p_sc[pl.ds(base, chunk), :] = dp
            m_sc[pl.ds(c, 1), :] = new
            return new, l, dl

        init = (
            jnp.full((1, tile), very_low, F32),
            jnp.zeros((1, tile), F32),
            jnp.zeros((1, tile), F32),
        )
        carry = lax.fori_loop(0, nfull, lambda c, x: scores(c, x, False), init)
        m, l, dl = scores(nfull, carry, True)
        inv = 1.0 / l
        delta = dl * inv

        def grads(c, acc):
            base = pl.multiple_of(c * chunk, chunk)
            f = jnp.exp2(m_sc[pl.ds(c, 1), :] - m) * inv
            p = e_sc[pl.ds(base, chunk), :] * f
            ds = (p * (p_sc[pl.ds(base, chunk), :] - delta)).astype(BF16)
            dk_sc[pl.ds(base, chunk), :] += dot_nn(ds, q)
            dv_sc[pl.ds(base, chunk), :] += dot_nn(p.astype(BF16), do)
            return acc + dot_tn(k_sc[pl.ds(base, chunk), :], ds)

        acc = lax.fori_loop(0, nfull + 1, grads, jnp.zeros((head_size, tile), F32))
        return (acc * scaling).T.astype(BF16)

    cut = rows * half // 2

    def put(dq):
        @pl.when(part == 0)
        def _():
            dq_ref[0, 0, 0, :cut, :] = dq[:cut]
            dq_ref[1, 0, 0, :cut, :] = dq[cut:]

        @pl.when(part > 0)
        def _():
            dq_ref[part - 1, 0, 0, cut:, :] = dq

    @pl.when(live)
    def _():
        put(run())

    @pl.when(jnp.logical_not(live))
    def _():
        put(jnp.zeros((tile, head_size), BF16))

    @pl.when(step == slots * per_slot - 1)
    def _():
        for j in range(blocks):
            at = pl.multiple_of(order[j] * rows, rows)
            dkv_ref[j, 0, 0, :rows, :] = (dk_sc[pl.ds(at, rows), :] * scaling).astype(BF16)
            dkv_ref[j, 1, 0, :rows, :] = dv_sc[pl.ds(at, rows), :].astype(BF16)
            dkv_ref[j, 0, 0, rows:, :] = (
                dk_sc[pl.ds(total + j * rows, rows), :] * scaling
            ).astype(BF16)
            dkv_ref[j, 1, 0, rows:, :] = dv_sc[pl.ds(total + j * rows, rows), :].astype(BF16)


def attention(order, lengths, qp, qr, dop, dor, key_value, head, first_block, side):
    slots, tile, size = qp.shape[1:]
    full_rows = qr.shape[2]
    blocks, _, heads, double, _ = key_value.shape
    rows = double // 2
    half = tile // rows
    full = full_rows // rows
    keys = blocks * double
    chunk = min(512, keys // 2)
    per_slot = 1 + full // half
    kern = functools.partial(
        attn_kernel,
        blocks=blocks,
        slots=slots,
        rows=rows,
        half=half,
        full=full,
        chunk=chunk,
        first_block=first_block,
        side=side,
    )
    out_rows = rows // 2 * (half + full)
    q_pref = pl.BlockSpec((1, 1, tile, size), lambda h, t, *_: (head + h, t // per_slot, 0, 0))
    q_resp = pl.BlockSpec(
        (1, 1, tile, size),
        lambda h, t, *_: (head + h, t // per_slot, jnp.maximum(t % per_slot - 1, 0), 0),
    )
    kv_spec = pl.BlockSpec((blocks, 2, 1, double, size), lambda h, t, *_: (0, 0, h, 0, 0))
    spec = pltpu.PrefetchScalarGridSpec(
        num_scalar_prefetch=2,
        grid=(heads, slots * per_slot),
        in_specs=[q_pref, q_resp, q_pref, q_resp, kv_spec],
        out_specs=[
            pl.BlockSpec(
                (2, 1, 1, out_rows, size), lambda h, t, *_: (0, t // per_slot, h, 0, 0)
            ),
            kv_spec,
        ],
        scratch_shapes=[
            pltpu.VMEM((tile, size), BF16),
            pltpu.VMEM((tile, size), BF16),
            pltpu.VMEM((keys, size), BF16),
            pltpu.VMEM((keys, size), BF16),
            pltpu.VMEM((keys, size), F32),
            pltpu.VMEM((keys, size), F32),
            pltpu.VMEM((keys, tile), F32),
            pltpu.VMEM((keys, tile), F32),
            pltpu.VMEM((keys // chunk, tile), F32),
        ],
    )
    work = heads * slots * per_slot * tile * keys
    return pl.pallas_call(
        kern,
        grid_spec=spec,
        out_shape=[
            jax.ShapeDtypeStruct((2, slots, heads, out_rows, size), BF16),
            jax.ShapeDtypeStruct(key_value.shape, BF16),
        ],
        compiler_params=pltpu.CompilerParams(vmem_limit_bytes=48 << 20),
        cost_estimate=pl.CostEstimate(
            flops=10 * work * size, bytes_accessed=8 * work // keys * size, transcendentals=work
        ),
    )(order, lengths, qp, qr, dop, dor, key_value)


def split_heads(array):
    rows, heads, group, size = array.shape
    return array.transpose(1, 0, 2, 3).reshape(heads, rows * group, size)


def on_device(
    prefix_query_rows,
    prefix_key_rows,
    prefix_value_rows,
    prefix_output_gradient,
    resp_q,
    resp_k,
    response_value_rows,
    response_output_gradient,
    lengths,
    prefix_order,
    *,
    swap,
):
    chips = lax.axis_size("z")
    cores = lax.axis_size("core")
    parts = lax.axis_size("head")
    rows, local_heads, half, size = prefix_query_rows.shape
    full = resp_q.shape[3]
    key_value = jnp.stack(
        [
            jnp.concatenate([prefix_key_rows, resp_k[0]], axis=0),
            jnp.concatenate([prefix_value_rows, response_value_rows[0]], axis=0),
        ]
    ).transpose(2, 0, 1, 3)
    arrays = [
        split_heads(prefix_query_rows),
        split_heads(resp_q[0]),
        split_heads(prefix_output_gradient),
        split_heads(response_output_gradient[0]),
    ]
    side = lambda: lax.axis_index("pair")
    slots = cores if swap else 1
    heads = local_heads // slots
    if swap:
        key_value = lax.all_to_all(key_value, "core", 0, 1, tiled=True)
        arrays = [lax.all_to_all(a, "core", 0, 1, tiled=True) for a in arrays]
        first_block = lambda: lax.axis_index("z") * cores
        over = "z"
    else:
        first_block = lambda: lax.axis_index("z") * cores + lax.axis_index("core")
        over = ("z", "core")
    arrays = [a.reshape(heads, slots, -1, size) for a in arrays]
    gathered = [
        lax.all_gather(key_value[g].reshape(slots, 2, 1, 2 * rows, size), over, axis=0, tiled=True)
        for g in range(heads)
    ]
    dqs = []
    dkvs = []
    for g in range(heads):
        dq, dkv = attention(
            prefix_order, lengths, *arrays, gathered[g], g, first_block, side
        )
        dkvs.append(lax.psum_scatter(dkv, over, scatter_dimension=0, tiled=True))
        dqs.append(dq)
    return finish(dqs, dkvs, rows, half, full, size, slots, parts, swap)


def finish(dqs, dkvs, rows, half, full, size, slots, parts, swap):
    heads = len(dqs)
    part = rows // parts
    axes = ("head", "core") if swap else "head"
    sources = parts * slots

    def exchange(array):
        return lax.all_to_all(array, axes, 0, 0, tiled=True)

    pref = []
    resp = []
    cut = rows * half // 2
    for dq in dqs:
        dq = dq.reshape(2, slots, -1, size)
        if parts == 2:
            got = exchange(dq.reshape(sources, -1, size))
            pref.append(got[:, :cut].reshape(sources, part, half, size))
            resp.append(got[:, cut:].reshape(sources, part, full, size))
        else:
            a = dq[:, 0, :cut].reshape(sources, part * half, size)
            b = dq[:, 0, cut:].reshape(sources, part * full, size)
            pref.append(exchange(a).reshape(sources, part, half, size))
            resp.append(exchange(b).reshape(sources, part, full, size))
    dq_pref = jnp.stack(pref, 1).transpose(2, 0, 1, 3, 4).reshape(part, -1, half, size)
    dq_resp = jnp.stack(resp, 1).transpose(2, 0, 1, 3, 4).reshape(part, -1, full, size)
    out = []
    sums = []
    for dkv in dkvs:
        dkv = dkv.reshape(slots, 2, 2, rows, size)
        own = dkv[:, :, 0]
        other = lax.ppermute(own, "pair", [(0, 1), (1, 0)])
        own = (own.astype(F32) + other.astype(F32)).astype(BF16)
        both = jnp.stack([own, dkv[:, :, 1]], axis=2)
        both = both.reshape(slots, 2, 2, parts, part, size)
        sums.append(both.transpose(3, 0, 1, 2, 4, 5))
    all_sums = jnp.stack(sums, axis=2)
    got = exchange(all_sums.reshape((sources,) + all_sums.shape[2:]))
    got = got.transpose(2, 3, 4, 0, 1, 5).reshape(2, 2, part, sources * heads, size)
    return (
        dq_pref,
        got[0, 0],
        got[1, 0],
        dq_resp[None],
        got[0, 1][None],
        got[1, 1][None],
    )


def solution(mesh):
    sizes = mesh.shape
    fine = Mesh(
        mesh.devices.reshape(sizes["blk"] // 2, 2, sizes["pair"], sizes["head"]),
        ("z", "core", "pair", "head"),
    )
    blk = ("z", "core")
    in_specs = (
        P(blk, "head", "pair", None),
        P(blk, "head", None),
        P(blk, "head", None),
        P(blk, "head", "pair", None),
        P("pair", blk, "head", None, None),
        P("pair", blk, "head", None),
        P("pair", blk, "head", None),
        P("pair", blk, "head", None, None),
        P(),
        P(),
    )
    rows = ("z", "core", "head")
    out_specs = (
        P(rows, None, "pair", None),
        P(rows, None, None),
        P(rows, None, None),
        P("pair", rows, None, None, None),
        P("pair", rows, None, None),
        P("pair", rows, None, None),
    )

    def run(*args):
        local_heads = args[1].shape[1] // sizes["head"]
        body = functools.partial(on_device, swap=local_heads % 2 == 0 and sizes["head"] == 2)
        return jax.shard_map(
            body, mesh=fine, in_specs=in_specs, out_specs=out_specs, check_vma=False
        )(*args)

    return run
```

```python
import functools
import math

import jax
import jax.numpy as jnp
from jax import lax
from jax.experimental import pallas as pl
from jax.experimental.pallas import tpu as pltpu
from jax.sharding import Mesh, PartitionSpec as P

F32 = jnp.float32
BF16 = jnp.bfloat16
very_low = -1e30


def dot_nt(a, b):
    return lax.dot_general(a, b, (((1,), (1,)), ((), ())), preferred_element_type=F32)


def dot_nn(a, b):
    return lax.dot_general(a, b, (((1,), (0,)), ((), ())), preferred_element_type=F32)


def dot_tn(a, b):
    return lax.dot_general(a, b, (((0,), (0,)), ((), ())), preferred_element_type=F32)


def attn_kernel(
    order,
    lengths,
    *refs,
    pieces,
    slots,
    rows,
    half,
    full,
    chunk,
    first_block,
    side,
):
    inputs = len(pieces)
    q_ref, do_ref = refs[:2]
    pref_refs = refs[2 : 2 + inputs]
    resp_refs = refs[2 + inputs : 2 + 2 * inputs]
    dq_ref, dkv_ref = refs[2 + 2 * inputs : 4 + 2 * inputs]
    k_sc, v_sc, dk_sc, dv_sc, e_sc, p_sc, m_sc = refs[4 + 2 * inputs :]
    step = pl.program_id(0)
    tile = rows * half
    per_slot = 1 + full // half
    slot = step // per_slot
    part = step % per_slot
    head_size = q_ref.shape[-1]
    scaling = head_size**-0.5
    cexp = scaling * math.log2(math.e)
    total = k_sc.shape[0] // 2
    blocks = total // rows
    block = first_block() + slot

    @pl.when(step == 0)
    def _():
        for (count, first), pref, resp in zip(pieces, pref_refs, resp_refs):
            for i in range(count):
                j = first() + i
                at = pl.multiple_of(order[j] * rows, rows)
                k_sc[pl.ds(at, rows), :] = pref[i, 0, 0]
                v_sc[pl.ds(at, rows), :] = pref[i, 1, 0]
                at = pl.multiple_of(total + j * rows, rows)
                k_sc[pl.ds(at, rows), :] = resp[i, 0, 0]
                v_sc[pl.ds(at, rows), :] = resp[i, 1, 0]
        dk_sc[...] = jnp.zeros_like(dk_sc)
        dv_sc[...] = jnp.zeros_like(dv_sc)

    sub = tile // full
    pos0 = jnp.where(part == 0, order[block] * rows, total + block * rows + (part - 1) * sub)
    shift = jnp.where(part == 0, int(math.log2(half)), int(math.log2(full)))
    live = jnp.logical_or(part == 0, block * rows < lengths[side()])
    nfull = (pos0 + 1) // chunk

    def run():
        q = q_ref[0, 0, 0]
        do = do_ref[0, 0, 0]

        def scores(c, carry, masked):
            m, l, dl = carry
            base = pl.multiple_of(c * chunk, chunk)
            s = dot_nt(k_sc[pl.ds(base, chunk), :], q) * cexp
            if masked:
                kp = base + lax.broadcasted_iota(jnp.int32, (chunk, tile), 0)
                qp = pos0 + lax.shift_right_logical(
                    lax.broadcasted_iota(jnp.int32, (chunk, tile), 1), shift
                )
                s = jnp.where(kp <= qp, s, very_low)
            new = jnp.maximum(m, jnp.max(s, axis=0, keepdims=True))
            e = jnp.exp2(s - new)
            dp = dot_nt(v_sc[pl.ds(base, chunk), :], do)
            a = jnp.exp2(m - new)
            l = l * a + jnp.sum(e, axis=0, keepdims=True)
            dl = dl * a + jnp.sum(e * dp, axis=0, keepdims=True)
            e_sc[pl.ds(base, chunk), :] = e
            p_sc[pl.ds(base, chunk), :] = dp
            m_sc[pl.ds(c, 1), :] = new
            return new, l, dl

        init = (
            jnp.full((1, tile), very_low, F32),
            jnp.zeros((1, tile), F32),
            jnp.zeros((1, tile), F32),
        )
        carry = lax.fori_loop(0, nfull, lambda c, x: scores(c, x, False), init)
        m, l, dl = scores(nfull, carry, True)
        inv = 1.0 / l
        delta = dl * inv

        def grads(c, acc):
            base = pl.multiple_of(c * chunk, chunk)
            f = jnp.exp2(m_sc[pl.ds(c, 1), :] - m) * inv
            p = e_sc[pl.ds(base, chunk), :] * f
            ds = (p * (p_sc[pl.ds(base, chunk), :] - delta)).astype(BF16)
            dk_sc[pl.ds(base, chunk), :] += dot_nn(ds, q)
            dv_sc[pl.ds(base, chunk), :] += dot_nn(p.astype(BF16), do)
            return acc + dot_tn(k_sc[pl.ds(base, chunk), :], ds)

        acc = lax.fori_loop(0, nfull + 1, grads, jnp.zeros((head_size, tile), F32))
        return (acc * scaling).T.astype(BF16)

    cut = tile // 2

    def put(dq):
        @pl.when(part == 0)
        def _():
            dq_ref[0, 0, :cut, :] = dq[:cut]
            dq_ref[1, 0, :cut, :] = dq[cut:]

        @pl.when(part > 0)
        def _():
            dq_ref[part - 1, 0, cut:, :] = dq

    @pl.when(live)
    def _():
        put(run())

    @pl.when(jnp.logical_not(live))
    def _():
        put(jnp.zeros((tile, head_size), BF16))

    @pl.when(step == slots * per_slot - 1)
    def _():
        parts, group = dkv_ref.shape[1:3]
        rows_out = rows // parts
        for j in range(blocks):
            for h in range(parts):
                at = pl.multiple_of(order[j] * rows + h * rows_out, rows_out)
                out = dkv_ref.at[j // group, h, j % group]
                out[0, 0] = (dk_sc[pl.ds(at, rows_out), :] * scaling).astype(BF16)
                out[1, 0] = dv_sc[pl.ds(at, rows_out), :].astype(BF16)
                at = total + j * rows + h * rows_out
                out[0, 1] = (dk_sc[pl.ds(at, rows_out), :] * scaling).astype(BF16)
                out[1, 1] = dv_sc[pl.ds(at, rows_out), :].astype(BF16)


def whole(shape):
    return pl.BlockSpec(shape, lambda *_: (0,) * len(shape))


def attention(order, lengths, q_do, head, prefs, resps, pieces, parts, group, half, full, first_block, side):
    slots = q_do.shape[1]
    size = q_do.shape[-1]
    rows = prefs[0].shape[3]
    blocks = order.shape[0]
    tile = rows * half
    keys = 2 * blocks * rows
    chunk = min(512, keys // 2)
    per_slot = 1 + full // half
    kern = functools.partial(
        attn_kernel,
        pieces=pieces,
        slots=slots,
        rows=rows,
        half=half,
        full=full,
        chunk=chunk,
        first_block=first_block,
        side=side,
    )
    out_rows = rows // 2 * (half + full)
    dkv_shape = (blocks // group, parts, group, 2, 2, rows // parts, size)

    def q_spec(which):
        return pl.BlockSpec(
            (1, 1, 1, tile, size),
            lambda t, *_: (head(), t // per_slot, which, t % per_slot, 0),
        )

    spec = pltpu.PrefetchScalarGridSpec(
        num_scalar_prefetch=2,
        grid=(slots * per_slot,),
        in_specs=[q_spec(0), q_spec(1)] + [whole(a.shape) for a in prefs + resps],
        out_specs=[
            pl.BlockSpec((2, 1, out_rows, size), lambda t, *_: (0, t // per_slot, 0, 0)),
            whole(dkv_shape),
        ],
        scratch_shapes=[
            pltpu.VMEM((keys, size), BF16),
            pltpu.VMEM((keys, size), BF16),
            pltpu.VMEM((keys, size), F32),
            pltpu.VMEM((keys, size), F32),
            pltpu.VMEM((keys, tile), F32),
            pltpu.VMEM((keys, tile), F32),
            pltpu.VMEM((keys // chunk, tile), F32),
        ],
    )
    work = slots * per_slot * tile * keys
    return pl.pallas_call(
        kern,
        grid_spec=spec,
        out_shape=[
            jax.ShapeDtypeStruct((2, slots, out_rows, size), BF16),
            jax.ShapeDtypeStruct(dkv_shape, BF16),
        ],
        compiler_params=pltpu.CompilerParams(vmem_limit_bytes=48 << 20),
        cost_estimate=pl.CostEstimate(
            flops=10 * work * size, bytes_accessed=16 << 20, transcendentals=work
        ),
    )(order, lengths, q_do, q_do, *prefs, *resps)


def split_heads(array):
    rows, heads, group, size = array.shape
    return array.transpose(1, 0, 2, 3).reshape(heads, rows * group, size)


def on_device(
    prefix_query_rows,
    prefix_key_rows,
    prefix_value_rows,
    prefix_output_gradient,
    resp_q,
    resp_k,
    response_value_rows,
    response_output_gradient,
    lengths,
    prefix_order,
    *,
    swap,
):
    rows, local_heads, half, size = prefix_query_rows.shape
    full = resp_q.shape[3]
    key_value = jnp.stack(
        [prefix_key_rows, resp_k[0], prefix_value_rows, response_value_rows[0]]
    ).reshape(2, 2, rows, local_heads, size)
    key_value = key_value.transpose(3, 0, 1, 2, 4)
    q_do = jnp.stack(
        [
            jnp.concatenate([split_heads(prefix_query_rows), split_heads(resp_q[0])], axis=1),
            jnp.concatenate(
                [split_heads(prefix_output_gradient), split_heads(response_output_gradient[0])],
                axis=1,
            ),
        ],
        axis=1,
    )
    side = lambda: lax.axis_index("pair")
    work = swapped if swap else gathered
    return work(key_value, q_do, lengths, prefix_order, rows, half, full, size, side)


def swapped(key_value, q_do, lengths, order, rows, half, full, size, side):
    chips = lax.axis_size("z")
    parts = lax.axis_size("head")
    heads = key_value.shape[0] // 2
    core = lax.axis_index("core")
    pair = lax.axis_index("pair")
    keep = lax.dynamic_slice_in_dim(key_value, core * heads, heads, 0)
    give = lax.dynamic_slice_in_dim(key_value, (1 - core) * heads, heads, 0)
    take = lax.ppermute(give, "core", [(0, 1), (1, 0)])
    mine = core == 0
    key_value = jnp.stack([jnp.where(mine, keep, take), jnp.where(mine, take, keep)], axis=1)
    q_do = lax.all_to_all(q_do[:, None], "core", 0, 1, tiled=True)

    def head_of(stage):
        return lambda: lax.bitwise_xor(lax.axis_index("pair"), stage)

    def pick(stage):
        return lax.dynamic_index_in_dim(key_value, head_of(stage)(), 0, keepdims=False)

    def along(array, k):
        return lax.ppermute(array, "z", [(i, i ^ k) for i in range(chips)])

    first, second = pick(0), pick(1)
    got = [first] + [along(first, k) for k in range(1, chips)]
    pref_one = [a[:, :, :1] for a in got]
    resp_one = [a[:, :, 1:] for a in got]
    own = second[:, :, 1:]
    resp_two = [own] + [along(own, k) for k in range(1, chips)]
    over = lax.ppermute(jnp.stack(pref_one[1:]), "pair", [(0, 1), (1, 0)])
    pref_two = [second[:, :, :1]] + [over[k] for k in range(chips - 1)]
    pieces = [
        (2, lambda k=k: 2 * lax.bitwise_xor(lax.axis_index("z"), k)) for k in range(chips)
    ]
    dqs = []
    sums = []
    for stage, (prefs, resps) in enumerate([(pref_one, resp_one), (pref_two, resp_two)]):
        with jax.named_scope(f"attn{stage}"):
            dq, dkv = attention(
                order,
                lengths,
                q_do,
                head_of(stage),
                prefs,
                resps,
                pieces,
                parts,
                2,
                half,
                full,
                pieces[0][1],
                side,
            )
        with jax.named_scope(f"dkv{stage}"):
            dkv = dkv.reshape((chips * parts * 2,) + dkv.shape[3:])
            dkv = lax.all_to_all(dkv, ("z", "head", "core"), 0, 0, tiled=True)
            dkv = dkv.reshape((chips, parts * 2) + dkv.shape[1:]).astype(F32)
            sums.append(jnp.sum(dkv, axis=0).astype(BF16))
        with jax.named_scope(f"dq{stage}"):
            dq = dq.reshape((parts * 2,) + dq.shape[2:])
            dqs.append(lax.all_to_all(dq, ("head", "core"), 0, 0, tiled=True))
    cut = rows * half // 2
    part = rows // parts
    straight = pair == 0

    def ordered(one, two, axis):
        return jnp.stack(
            [jnp.where(straight, one, two), jnp.where(straight, two, one)], axis=axis
        )

    pref = ordered(*[d[:, :cut].reshape(-1, part, half, size) for d in dqs], 1)
    resp = ordered(*[d[:, cut:].reshape(-1, part, full, size) for d in dqs], 1)
    dq_pref = pref.transpose(2, 0, 1, 3, 4).reshape(part, -1, half, size)
    dq_resp = resp.transpose(2, 0, 1, 3, 4).reshape(part, -1, full, size)
    others = [lax.ppermute(s[:, :, 0], "pair", [(0, 1), (1, 0)]).astype(F32) for s in sums]
    both = [
        (sums[i][:, :, 0].astype(F32) + others[1 - i]).astype(BF16) for i in range(2)
    ]
    pref = ordered(*both, 1)
    resp = ordered(*[s[:, :, 1] for s in sums], 1)
    pref = pref.transpose(2, 3, 0, 1, 4).reshape(2, part, -1, size)
    resp = resp.transpose(2, 3, 0, 1, 4).reshape(2, part, -1, size)
    return (dq_pref, pref[0], pref[1], dq_resp[None], resp[0][None], resp[1][None])


def gathered(key_value, q_do, lengths, order, rows, half, full, size, side):
    parts = lax.axis_size("head")
    blk = ("z", "core")
    cores = lax.axis_size("core")
    heads = key_value.shape[0]
    part = rows // parts
    cut = rows * half // 2
    mine = lambda: lax.axis_index("z") * cores + lax.axis_index("core")
    pref_q, resp_q, pref_kv, resp_kv = [], [], [], []

    def exchange(array):
        return lax.all_to_all(array, "head", 0, 0, tiled=True)

    for g in range(heads):
        kv = lax.all_gather(key_value[g], blk, axis=0)
        dq, dkv = attention(
            order,
            lengths,
            q_do[:, None],
            lambda g=g: g,
            [kv[:, :, :1]],
            [kv[:, :, 1:]],
            [(kv.shape[0], lambda: 0)],
            1,
            1,
            half,
            full,
            mine,
            side,
        )
        dkv = lax.psum_scatter(dkv, blk, scatter_dimension=0, tiled=True)
        dkv = dkv.reshape(2, 2, rows, size)
        own = lax.psum(dkv[:, 0].astype(F32), "pair").astype(BF16)
        pref_q.append(exchange(dq[:, 0, :cut].reshape(parts, part, half, size)))
        resp_q.append(exchange(dq[:, 0, cut:].reshape(parts, part, full, size)))
        pref_kv.append(exchange(own.reshape(2, parts, part, size).transpose(1, 0, 2, 3)))
        resp_kv.append(exchange(dkv[:, 1].reshape(2, parts, part, size).transpose(1, 0, 2, 3)))
    dq_pref = jnp.stack(pref_q, 1).transpose(2, 0, 1, 3, 4).reshape(part, -1, half, size)
    dq_resp = jnp.stack(resp_q, 1).transpose(2, 0, 1, 3, 4).reshape(part, -1, full, size)
    pref = jnp.stack(pref_kv, 1).transpose(2, 3, 0, 1, 4).reshape(2, part, -1, size)
    resp = jnp.stack(resp_kv, 1).transpose(2, 3, 0, 1, 4).reshape(2, part, -1, size)
    return (dq_pref, pref[0], pref[1], dq_resp[None], resp[0][None], resp[1][None])


def swap(local_heads, sizes):
    chips = sizes["blk"] // 2
    return local_heads == 4 and sizes["head"] == 2 and chips & (chips - 1) == 0


def solution(mesh):
    sizes = mesh.shape
    fine = Mesh(
        mesh.devices.reshape(sizes["blk"] // 2, 2, sizes["pair"], sizes["head"]),
        ("z", "core", "pair", "head"),
    )
    blk = ("z", "core")
    in_specs = (
        P(blk, "head", "pair", None),
        P(blk, "head", None),
        P(blk, "head", None),
        P(blk, "head", "pair", None),
        P("pair", blk, "head", None, None),
        P("pair", blk, "head", None),
        P("pair", blk, "head", None),
        P("pair", blk, "head", None, None),
        P(),
        P(),
    )
    rows = ("z", "core", "head")
    out_specs = (
        P(rows, None, "pair", None),
        P(rows, None, None),
        P(rows, None, None),
        P("pair", rows, None, None, None),
        P("pair", rows, None, None),
        P("pair", rows, None, None),
    )

    def run(*args):
        local_heads = args[1].shape[1] // sizes["head"]
        body = functools.partial(on_device, swap=swap(local_heads, sizes))
        return jax.shard_map(
            body, mesh=fine, in_specs=in_specs, out_specs=out_specs, check_vma=False
        )(*args)

    return run
```

```python
import functools
import math

import jax
import jax.numpy as jnp
from jax import lax
from jax.experimental import pallas as pl
from jax.experimental.pallas import tpu as pltpu
from jax.sharding import Mesh, PartitionSpec as P

F32 = jnp.float32
BF16 = jnp.bfloat16
very_low = -1e30


def dot_nt(a, b):
    return lax.dot_general(a, b, (((1,), (1,)), ((), ())), preferred_element_type=F32)


def dot_nn(a, b):
    return lax.dot_general(a, b, (((1,), (0,)), ((), ())), preferred_element_type=F32)


def dot_tn(a, b):
    return lax.dot_general(a, b, (((0,), (0,)), ((), ())), preferred_element_type=F32)


def attn_kernel(
    order,
    lengths,
    *refs,
    pieces,
    inputs,
    slots,
    rows,
    half,
    full,
    chunk,
    first_block,
    side,
    flip,
):
    q_ref, do_ref = refs[:2]
    kv_refs = refs[2 : 2 + inputs]
    dq_refs = refs[2 + inputs : 2 + inputs + 2 * slots]
    dkv_ref, k_sc, v_sc, dk_sc, dv_sc, e_sc, p_sc, m_sc = refs[2 + inputs + 2 * slots :]
    step = pl.program_id(0)
    tile = rows * half
    per_slot = 1 + full // half
    slot = step // per_slot
    part = step % per_slot
    head_size = q_ref.shape[-1]
    scaling = head_size**-0.5
    cexp = scaling * math.log2(math.e)
    total = k_sc.shape[0] // 2
    blocks = total // rows
    block = first_block() + slot

    @pl.when(step == 0)
    def _():
        for count, first, pref, resp in pieces:
            for i in range(count):
                j = first() + i
                for kind, at in ((pref, order[j] * rows), (resp, total + j * rows)):
                    array, lead = kind
                    at = pl.multiple_of(at, rows)
                    k_sc[pl.ds(at, rows), :] = kv_refs[array][lead + (i, 0)]
                    v_sc[pl.ds(at, rows), :] = kv_refs[array][lead + (i, 1)]
        dk_sc[...] = jnp.zeros_like(dk_sc)
        dv_sc[...] = jnp.zeros_like(dv_sc)

    sub = tile // full
    pos0 = jnp.where(part == 0, order[block] * rows, total + block * rows + (part - 1) * sub)
    shift = jnp.where(part == 0, int(math.log2(half)), int(math.log2(full)))
    live = jnp.logical_or(part == 0, block * rows < lengths[side()])
    nfull = (pos0 + 1) // chunk

    def run():
        q = q_ref[0, 0, 0]
        do = do_ref[0, 0, 0]

        def scores(c, carry, masked):
            m, l, dl = carry
            base = pl.multiple_of(c * chunk, chunk)
            s = dot_nt(k_sc[pl.ds(base, chunk), :], q) * cexp
            if masked:
                kp = base + lax.broadcasted_iota(jnp.int32, (chunk, tile), 0)
                qp = pos0 + lax.shift_right_logical(
                    lax.broadcasted_iota(jnp.int32, (chunk, tile), 1), shift
                )
                s = jnp.where(kp <= qp, s, very_low)
            new = jnp.maximum(m, jnp.max(s, axis=0, keepdims=True))
            e = jnp.exp2(s - new)
            dp = dot_nt(v_sc[pl.ds(base, chunk), :], do)
            a = jnp.exp2(m - new)
            l = l * a + jnp.sum(e, axis=0, keepdims=True)
            dl = dl * a + jnp.sum(e * dp, axis=0, keepdims=True)
            e_sc[pl.ds(base, chunk), :] = e
            p_sc[pl.ds(base, chunk), :] = dp
            m_sc[pl.ds(c, 1), :] = new
            return new, l, dl

        init = (
            jnp.full((1, tile), very_low, F32),
            jnp.zeros((1, tile), F32),
            jnp.zeros((1, tile), F32),
        )
        carry = lax.fori_loop(0, nfull, lambda c, x: scores(c, x, False), init)
        m, l, dl = scores(nfull, carry, True)
        inv = 1.0 / l
        delta = dl * inv

        def grads(c, acc):
            base = pl.multiple_of(c * chunk, chunk)
            f = jnp.exp2(m_sc[pl.ds(c, 1), :] - m) * inv
            p = e_sc[pl.ds(base, chunk), :] * f
            ds = (p * (p_sc[pl.ds(base, chunk), :] - delta)).astype(BF16)
            dk_sc[pl.ds(base, chunk), :] += dot_nn(ds, q)
            dv_sc[pl.ds(base, chunk), :] += dot_nn(p.astype(BF16), do)
            return acc + dot_tn(k_sc[pl.ds(base, chunk), :], ds)

        acc = lax.fori_loop(0, nfull + 1, grads, jnp.zeros((head_size, tile), F32))
        return (acc * scaling).T.astype(BF16)

    cut = tile // 2

    def put(dq):
        for index, ref in enumerate(dq_refs):
            mine = (slot ^ flip()[1]) == index % slots
            at = (index // slots) ^ flip()[0]

            @pl.when(jnp.logical_and(mine, part == 0))
            def _(ref=ref, at=at):
                ref[:cut, :] = jnp.where(at == 0, dq[:cut], dq[cut:])

            @pl.when(jnp.logical_and(mine, part == 1 + at))
            def _(ref=ref):
                ref[cut:, :] = dq

    @pl.when(live)
    def _():
        put(run())

    @pl.when(jnp.logical_not(live))
    def _():
        put(jnp.zeros((tile, head_size), BF16))

    @pl.when(step == slots * per_slot - 1)
    def _():
        parts, group = dkv_ref.shape[1:3]
        rows_out = rows // parts
        for j in range(blocks):
            for h in range(parts):
                at = pl.multiple_of(order[j] * rows + h * rows_out, rows_out)
                out = dkv_ref.at[j // group, h, j % group]
                out[0, 0] = (dk_sc[pl.ds(at, rows_out), :] * scaling).astype(BF16)
                out[1, 0] = dv_sc[pl.ds(at, rows_out), :].astype(BF16)
                at = total + j * rows + h * rows_out
                out[0, 1] = (dk_sc[pl.ds(at, rows_out), :] * scaling).astype(BF16)
                out[1, 1] = dv_sc[pl.ds(at, rows_out), :].astype(BF16)


def whole(shape):
    return pl.BlockSpec(shape, lambda *_: (0,) * len(shape))


def attention(order, lengths, q_do, head, arrays, pieces, parts, group, half, full, first_block, side, flip):
    slots = q_do.shape[1]
    size = q_do.shape[-1]
    rows = arrays[0].shape[-2]
    blocks = order.shape[0]
    tile = rows * half
    keys = 2 * blocks * rows
    chunk = min(1024, keys // 2)
    per_slot = 1 + full // half
    kern = functools.partial(
        attn_kernel,
        pieces=pieces,
        inputs=len(arrays),
        slots=slots,
        rows=rows,
        half=half,
        full=full,
        chunk=chunk,
        first_block=first_block,
        side=side,
        flip=flip,
    )
    out_rows = rows // 2 * (half + full)
    dkv_shape = (blocks // group, parts, group, 2, 2, rows // parts, size)

    def q_spec(which):
        return pl.BlockSpec(
            (1, 1, 1, tile, size),
            lambda t, *_: (head(), t // per_slot, which, t % per_slot, 0),
        )

    spec = pltpu.PrefetchScalarGridSpec(
        num_scalar_prefetch=2,
        grid=(slots * per_slot,),
        in_specs=[q_spec(0), q_spec(1)] + [whole(a.shape) for a in arrays],
        out_specs=[whole((out_rows, size))] * (2 * slots) + [whole(dkv_shape)],
        scratch_shapes=[
            pltpu.VMEM((keys, size), BF16),
            pltpu.VMEM((keys, size), BF16),
            pltpu.VMEM((keys, size), F32),
            pltpu.VMEM((keys, size), F32),
            pltpu.VMEM((keys, tile), F32),
            pltpu.VMEM((keys, tile), F32),
            pltpu.VMEM((keys // chunk, tile), F32),
        ],
    )
    work = slots * per_slot * tile * keys
    return pl.pallas_call(
        kern,
        grid_spec=spec,
        out_shape=[jax.ShapeDtypeStruct((out_rows, size), BF16)] * (2 * slots)
        + [jax.ShapeDtypeStruct(dkv_shape, BF16)],
        compiler_params=pltpu.CompilerParams(vmem_limit_bytes=62 << 20),
        cost_estimate=pl.CostEstimate(
            flops=10 * work * size, bytes_accessed=16 << 20, transcendentals=work
        ),
    )(order, lengths, q_do, q_do, *arrays)


def split_heads(array):
    rows, heads, group, size = array.shape
    return array.transpose(1, 0, 2, 3).reshape(heads, rows * group, size)


def on_device(
    prefix_query_rows,
    prefix_key_rows,
    prefix_value_rows,
    prefix_output_gradient,
    resp_q,
    resp_k,
    response_value_rows,
    response_output_gradient,
    lengths,
    prefix_order,
    *,
    swap,
):
    rows, local_heads, half, size = prefix_query_rows.shape
    full = resp_q.shape[3]
    key_value = jnp.stack(
        [prefix_key_rows, prefix_value_rows, resp_k[0], response_value_rows[0]]
    ).reshape(2, 2, rows, local_heads, size)
    key_value = key_value.transpose(3, 0, 1, 2, 4)
    queries = (
        prefix_query_rows,
        resp_q[0],
        prefix_output_gradient,
        response_output_gradient[0],
    )
    side = lambda: lax.axis_index("pair")
    work = swapped if swap else gathered
    return work(key_value, queries, lengths, prefix_order, rows, half, full, size, side)


def join_queries(queries):
    parts = [split_heads(a) for a in queries]
    return jnp.stack(
        [jnp.concatenate(parts[:2], axis=1), jnp.concatenate(parts[2:], axis=1)], axis=1
    )


def swapped(key_value, queries, lengths, order, rows, half, full, size, side):
    chips = lax.axis_size("z")
    parts = lax.axis_size("head")
    heads = key_value.shape[0] // 2
    core = lax.axis_index("core")
    pair = lax.axis_index("pair")
    keep = lax.dynamic_slice_in_dim(key_value, core * heads, heads, 0)
    give = lax.dynamic_slice_in_dim(key_value, (1 - core) * heads, heads, 0)
    take = lax.ppermute(give, "core", [(0, 1), (1, 0)])
    mine = core == 0
    key_value = jnp.stack([jnp.where(mine, keep, take), jnp.where(mine, take, keep)], axis=2)

    def head_of(stage):
        return lambda: lax.bitwise_xor(lax.axis_index("pair"), stage)

    def pick(stage):
        return lax.dynamic_index_in_dim(key_value, head_of(stage)(), 0, keepdims=False)

    def along(array, k):
        return lax.ppermute(array, "z", [(i, i ^ k) for i in range(chips)])

    first, second = pick(0), pick(1)
    first, second, queries = lax.optimization_barrier((first, second, queries))
    q_do = join_queries(queries)[:, None]
    q_do = lax.all_to_all(q_do, "core", 0, 1, tiled=True)
    far = range(chips - 1, 0, -1)
    one = {k: along(first, k) for k in far}
    two = {k: along(second[1], k) for k in far}
    over = lax.ppermute(
        jnp.stack([one[k][0] for k in far]), "pair", [(0, 1), (1, 0)]
    )

    def block(k):
        return lambda: 2 * lax.bitwise_xor(lax.axis_index("z"), k)

    stages = [
        (
            [first] + [one[k] for k in far],
            [(2, block(0), (0, (0,)), (0, (1,)))]
            + [(2, block(k), (i + 1, (0,)), (i + 1, (1,))) for i, k in enumerate(far)],
        ),
        (
            [second] + [two[k] for k in far] + [over],
            [(2, block(0), (0, (0,)), (0, (1,)))]
            + [(2, block(k), (chips, (i,)), (i + 1, ())) for i, k in enumerate(far)],
        ),
    ]
    dqs = []
    sums = []
    others = []
    for stage, (arrays, pieces) in enumerate(stages):
        *dq, dkv = attention(
            order,
            lengths,
            q_do,
            head_of(stage),
            arrays,
            pieces,
            parts,
            2,
            half,
            full,
            pieces[0][1],
            side,
            lambda: (lax.axis_index("head"), lax.axis_index("core")),
        )
        dkv = dkv.reshape((chips * parts * 2,) + dkv.shape[3:])
        dkv = lax.all_to_all(dkv, ("z", "head", "core"), 0, 0, tiled=True)
        if others:
            dkv, others[0] = lax.optimization_barrier((dkv, others[0]))
        dkv = dkv.reshape((chips, parts * 2) + dkv.shape[1:]).astype(F32)
        sums.append(jnp.sum(dkv, axis=0).astype(BF16))
        others.append(lax.ppermute(sums[stage][:, :, 0], "pair", [(0, 1), (1, 0)]))
        moved = dq[:1]
        for k in range(1, 4):
            to = 2 * (k % 2) + k // 2
            moved.append(
                lax.ppermute(dq[k], ("core", "head"), [(i, i ^ to) for i in range(4)])
            )
        dqs.append(moved)
    cut = rows * half // 2
    part = rows // parts
    straight = pair == 0

    def ordered(one, two, axis):
        return jnp.stack(
            [jnp.where(straight, one, two), jnp.where(straight, two, one)], axis=axis
        )

    index = 2 * lax.axis_index("head") + core

    def sorted_by_source(moved):
        a, b, c, d = [jnp.where(core == 0, moved[i], moved[i ^ 1]) for i in range(4)]
        low = index < 2
        return jnp.stack(
            [jnp.where(low, a, c), jnp.where(low, b, d), jnp.where(low, c, a), jnp.where(low, d, b)]
        )

    dqs = [sorted_by_source(moved) for moved in dqs]
    pref = ordered(*[d[:, :cut].reshape(-1, part, half, size) for d in dqs], 1)
    resp = ordered(*[d[:, cut:].reshape(-1, part, full, size) for d in dqs], 1)
    dq_pref = pref.transpose(2, 0, 1, 3, 4).reshape(part, -1, half, size)
    dq_resp = resp.transpose(2, 0, 1, 3, 4).reshape(part, -1, full, size)
    both = [
        (sums[i][:, :, 0].astype(F32) + others[1 - i].astype(F32)).astype(BF16) for i in range(2)
    ]
    pref = ordered(*both, 1)
    resp = ordered(*[s[:, :, 1] for s in sums], 1)
    pref = pref.transpose(2, 3, 0, 1, 4).reshape(2, part, -1, size)
    resp = resp.transpose(2, 3, 0, 1, 4).reshape(2, part, -1, size)
    return (dq_pref, pref[0], pref[1], dq_resp[None], resp[0][None], resp[1][None])


def gathered(key_value, queries, lengths, order, rows, half, full, size, side):
    q_do = join_queries(queries)
    parts = lax.axis_size("head")
    blk = ("z", "core")
    cores = lax.axis_size("core")
    heads = key_value.shape[0]
    part = rows // parts
    cut = rows * half // 2
    mine = lambda: lax.axis_index("z") * cores + lax.axis_index("core")
    pref_q, resp_q, pref_kv, resp_kv = [], [], [], []

    def exchange(array):
        return lax.all_to_all(array, "head", 0, 0, tiled=True)

    for g in range(heads):
        kv = lax.all_gather(key_value[g], blk, axis=1)
        *dq, dkv = attention(
            order,
            lengths,
            q_do[:, None],
            lambda g=g: g,
            [kv],
            [(kv.shape[1], lambda: 0, (0, (0,)), (0, (1,)))],
            1,
            1,
            half,
            full,
            mine,
            side,
            lambda: (0, 0),
        )
        dq = jnp.stack(dq)
        dkv = lax.psum_scatter(dkv, blk, scatter_dimension=0, tiled=True)
        dkv = dkv.reshape(2, 2, rows, size)
        own = lax.psum(dkv[:, 0].astype(F32), "pair").astype(BF16)
        pref_q.append(exchange(dq[:, :cut].reshape(parts, part, half, size)))
        resp_q.append(exchange(dq[:, cut:].reshape(parts, part, full, size)))
        pref_kv.append(exchange(own.reshape(2, parts, part, size).transpose(1, 0, 2, 3)))
        resp_kv.append(exchange(dkv[:, 1].reshape(2, parts, part, size).transpose(1, 0, 2, 3)))
    dq_pref = jnp.stack(pref_q, 1).transpose(2, 0, 1, 3, 4).reshape(part, -1, half, size)
    dq_resp = jnp.stack(resp_q, 1).transpose(2, 0, 1, 3, 4).reshape(part, -1, full, size)
    pref = jnp.stack(pref_kv, 1).transpose(2, 3, 0, 1, 4).reshape(2, part, -1, size)
    resp = jnp.stack(resp_kv, 1).transpose(2, 3, 0, 1, 4).reshape(2, part, -1, size)
    return (dq_pref, pref[0], pref[1], dq_resp[None], resp[0][None], resp[1][None])


def swap(local_heads, sizes):
    chips = sizes["blk"] // 2
    return local_heads == 4 and sizes["head"] == 2 and chips & (chips - 1) == 0


def solution(mesh):
    sizes = mesh.shape
    fine = Mesh(
        mesh.devices.reshape(sizes["blk"] // 2, 2, sizes["pair"], sizes["head"]),
        ("z", "core", "pair", "head"),
    )
    blk = ("z", "core")
    in_specs = (
        P(blk, "head", "pair", None),
        P(blk, "head", None),
        P(blk, "head", None),
        P(blk, "head", "pair", None),
        P("pair", blk, "head", None, None),
        P("pair", blk, "head", None),
        P("pair", blk, "head", None),
        P("pair", blk, "head", None, None),
        P(),
        P(),
    )
    rows = ("z", "core", "head")
    out_specs = (
        P(rows, None, "pair", None),
        P(rows, None, None),
        P(rows, None, None),
        P("pair", rows, None, None, None),
        P("pair", rows, None, None),
        P("pair", rows, None, None),
    )

    def run(*args):
        local_heads = args[1].shape[1] // sizes["head"]
        body = functools.partial(on_device, swap=swap(local_heads, sizes))
        step = jax.shard_map(
            body, mesh=fine, in_specs=in_specs, out_specs=out_specs, check_vma=False
        )
        return step(*args)

    return run
```

```python
import functools
import math

import jax
import jax.numpy as jnp
from jax import lax
from jax.experimental import pallas as pl
from jax.experimental.pallas import tpu as pltpu
from jax.sharding import Mesh, PartitionSpec as P

F32 = jnp.float32
BF16 = jnp.bfloat16
very_low = -1e30


def dot_nt(a, b):
    return lax.dot_general(a, b, (((1,), (1,)), ((), ())), preferred_element_type=F32)


def dot_nn(a, b):
    return lax.dot_general(a, b, (((1,), (0,)), ((), ())), preferred_element_type=F32)


def dot_tn(a, b):
    return lax.dot_general(a, b, (((0,), (0,)), ((), ())), preferred_element_type=F32)


def attn_kernel(
    order,
    lengths,
    *refs,
    pieces,
    inputs,
    slots,
    rows,
    half,
    full,
    first_block,
    side,
    flip,
):
    q_ref, do_ref = refs[:2]
    kv_refs = refs[2 : 2 + inputs]
    dq_refs = refs[2 + inputs : 2 + inputs + 2 * slots]
    dkv_ref, k_sc, v_sc, dk_sc, dv_sc, e_sc, p_sc, dq_sc = refs[2 + inputs + 2 * slots :]
    step = pl.program_id(0)
    head_size = q_ref.shape[-1]
    scaling = head_size**-0.5
    cexp = scaling * math.log2(math.e)
    total = k_sc.shape[0] // 2
    blocks = total // rows
    cut = rows * half

    @pl.when(step == 0)
    def _():
        for count, first, pref, resp in pieces:
            for i in range(count):
                j = first() + i
                for kind, at in ((pref, order[j] * rows), (resp, total + j * rows)):
                    array, lead = kind
                    at = pl.multiple_of(at, rows)
                    k_sc[pl.ds(at, rows), :] = kv_refs[array][lead + (i, 0)]
                    v_sc[pl.ds(at, rows), :] = kv_refs[array][lead + (i, 1)]
        dk_sc[...] = jnp.zeros_like(dk_sc)
        dv_sc[...] = jnp.zeros_like(dv_sc)

    def run(q, do, query_pos, chunks):
        tile = q.shape[0]
        parts = []
        for base, size, free in chunks:
            s = dot_nt(k_sc[base : base + size, :], q) * cexp
            if free < size:
                kp = base + free + lax.broadcasted_iota(jnp.int32, (size - free, tile), 0)
                tail = jnp.where(kp <= query_pos, s[free:], very_low)
                s = jnp.concatenate([s[:free], tail], axis=0) if free else tail
            dp = dot_nt(v_sc[base : base + size, :], do)
            m = jnp.max(s, axis=0, keepdims=True)
            e = jnp.exp2(s - m)
            e_sc[base : base + size, :tile] = e
            p_sc[base : base + size, :tile] = dp
            parts.append(
                (m, jnp.sum(e, axis=0, keepdims=True), jnp.sum(e * dp, axis=0, keepdims=True))
            )
        top = parts[0][0]
        for m, _, _ in parts[1:]:
            top = jnp.maximum(top, m)
        factors = [jnp.exp2(m - top) for m, _, _ in parts]
        inv = 1.0 / sum(f * l for f, (_, l, _) in zip(factors, parts))
        delta = sum(f * d for f, (_, _, d) in zip(factors, parts)) * inv
        acc = 0.0
        for f, (base, size, _) in zip(factors, chunks):
            p = e_sc[base : base + size, :tile] * (f * inv)
            ds = (p * (p_sc[base : base + size, :tile] - delta)).astype(BF16)
            dk_sc[base : base + size, :] += dot_nn(ds, q)
            dv_sc[base : base + size, :] += dot_nn(p.astype(BF16), do)
            acc = acc + dot_tn(k_sc[base : base + size, :], ds)
        return (acc * scaling).T.astype(BF16)

    @pl.when(step == 0)
    def _():
        def rows_of(ref):
            return jnp.concatenate([ref[0, i, 0, :cut] for i in range(slots)], axis=0)

        row = lax.broadcasted_iota(jnp.int32, (1, slots * cut), 1)
        offset = lax.shift_right_logical(row, int(math.log2(half)))
        pos = offset + order[first_block()] * rows
        for i in range(1, slots):
            here = offset - i * rows + order[first_block() + i] * rows
            pos = jnp.where(row < i * cut, pos, here)
        dq = run(rows_of(q_ref), rows_of(do_ref), pos, [(0, total, 0)])
        dq_sc[: slots * cut, :] = dq
        for index, ref in enumerate(dq_refs):
            at = (index % slots ^ flip()[1]) * cut + (index // slots ^ flip()[0]) * (cut // 2)
            ref[: cut // 2, :] = dq_sc[pl.ds(pl.multiple_of(at, cut // 2), cut // 2), :]

    @pl.when(step > 0)
    def _():
        slot = step - 1
        block = first_block() + slot
        tile = rows * full
        live = block * rows < lengths[side()]

        @pl.when(live)
        def _():
            row = lax.broadcasted_iota(jnp.int32, (1, tile), 1)
            pos = total + block * rows + lax.shift_right_logical(row, int(math.log2(full)))
            if 2 * total <= 2048:
                chunks = [(0, 2 * total, total)]
            else:
                chunks = [(at, 1024, 1024 if at < total else 0) for at in range(0, 2 * total, 1024)]
            dq_sc[:tile, :] = run(
                q_ref[0, slot, 0, pl.ds(cut, tile)], do_ref[0, slot, 0, pl.ds(cut, tile)], pos, chunks
            )

        @pl.when(jnp.logical_not(live))
        def _():
            dq_sc[:tile, :] = jnp.zeros((tile, head_size), BF16)

        for index, ref in enumerate(dq_refs):

            @pl.when(slot == index % slots ^ flip()[1])
            def _(index=index, ref=ref):
                at = (index // slots ^ flip()[0]) * (tile // 2)
                ref[cut // 2 :, :] = dq_sc[pl.ds(pl.multiple_of(at, tile // 2), tile // 2), :]

    @pl.when(step == slots)
    def _():
        parts, group = dkv_ref.shape[1:3]
        rows_out = rows // parts
        for j in range(blocks):
            for h in range(parts):
                at = pl.multiple_of(order[j] * rows + h * rows_out, rows_out)
                out = dkv_ref.at[j // group, h, j % group]
                out[0, 0] = (dk_sc[pl.ds(at, rows_out), :] * scaling).astype(BF16)
                out[1, 0] = dv_sc[pl.ds(at, rows_out), :].astype(BF16)
                at = total + j * rows + h * rows_out
                out[0, 1] = (dk_sc[pl.ds(at, rows_out), :] * scaling).astype(BF16)
                out[1, 1] = dv_sc[pl.ds(at, rows_out), :].astype(BF16)


def whole(shape):
    return pl.BlockSpec(shape, lambda *_: (0,) * len(shape))


def attention(order, lengths, q_do, head, arrays, pieces, parts, group, half, full, first_block, side, flip):
    slots = q_do.shape[1]
    size = q_do.shape[-1]
    rows = arrays[0].shape[-2]
    blocks = order.shape[0]
    tile = rows * max(slots * half, full)
    keys = 2 * blocks * rows
    kern = functools.partial(
        attn_kernel,
        pieces=pieces,
        inputs=len(arrays),
        slots=slots,
        rows=rows,
        half=half,
        full=full,
        first_block=first_block,
        side=side,
        flip=flip,
    )
    out_rows = rows // 2 * (half + full)
    dkv_shape = (blocks // group, parts, group, 2, 2, rows // parts, size)

    def q_spec(which):
        return pl.BlockSpec(
            (1, slots, 1, rows * (half + full), size), lambda t, *_: (head(), 0, which, 0, 0)
        )

    spec = pltpu.PrefetchScalarGridSpec(
        num_scalar_prefetch=2,
        grid=(1 + slots,),
        in_specs=[q_spec(0), q_spec(1)] + [whole(a.shape) for a in arrays],
        out_specs=[whole((out_rows, size))] * (2 * slots) + [whole(dkv_shape)],
        scratch_shapes=[
            pltpu.VMEM((keys, size), BF16),
            pltpu.VMEM((keys, size), BF16),
            pltpu.VMEM((keys, size), F32),
            pltpu.VMEM((keys, size), F32),
            pltpu.VMEM((keys, tile), F32),
            pltpu.VMEM((keys, tile), F32),
            pltpu.VMEM((tile, size), BF16),
        ],
    )
    work = slots * rows * (full + half // 2) * keys
    return pl.pallas_call(
        kern,
        grid_spec=spec,
        out_shape=[jax.ShapeDtypeStruct((out_rows, size), BF16)] * (2 * slots)
        + [jax.ShapeDtypeStruct(dkv_shape, BF16)],
        compiler_params=pltpu.CompilerParams(vmem_limit_bytes=62 << 20),
        cost_estimate=pl.CostEstimate(
            flops=10 * work * size, bytes_accessed=16 << 20, transcendentals=work
        ),
    )(order, lengths, q_do, q_do, *arrays)


def split_heads(array):
    rows, heads, group, size = array.shape
    return array.transpose(1, 0, 2, 3).reshape(heads, rows * group, size)


def on_device(
    prefix_query_rows,
    prefix_key_rows,
    prefix_value_rows,
    prefix_output_gradient,
    resp_q,
    resp_k,
    response_value_rows,
    response_output_gradient,
    lengths,
    prefix_order,
    *,
    swap,
):
    rows, local_heads, half, size = prefix_query_rows.shape
    full = resp_q.shape[3]
    key_value = jnp.stack(
        [prefix_key_rows, prefix_value_rows, resp_k[0], response_value_rows[0]]
    ).reshape(2, 2, rows, local_heads, size)
    key_value = key_value.transpose(3, 0, 1, 2, 4)
    queries = (
        prefix_query_rows,
        resp_q[0],
        prefix_output_gradient,
        response_output_gradient[0],
    )
    side = lambda: lax.axis_index("pair")
    work = swapped if swap else gathered
    return work(key_value, queries, lengths, prefix_order, rows, half, full, size, side)


def join_queries(queries):
    parts = [split_heads(a) for a in queries]
    return jnp.stack(
        [jnp.concatenate(parts[:2], axis=1), jnp.concatenate(parts[2:], axis=1)], axis=1
    )


def swapped(key_value, queries, lengths, order, rows, half, full, size, side):
    chips = lax.axis_size("z")
    parts = lax.axis_size("head")
    heads = key_value.shape[0] // 2
    core = lax.axis_index("core")
    pair = lax.axis_index("pair")
    keep = lax.dynamic_slice_in_dim(key_value, core * heads, heads, 0)
    give = lax.dynamic_slice_in_dim(key_value, (1 - core) * heads, heads, 0)
    take = lax.ppermute(give, "core", [(0, 1), (1, 0)])
    mine = core == 0
    key_value = jnp.stack([jnp.where(mine, keep, take), jnp.where(mine, take, keep)], axis=2)

    def head_of(stage):
        return lambda: lax.bitwise_xor(lax.axis_index("pair"), stage)

    def pick(stage):
        return lax.dynamic_index_in_dim(key_value, head_of(stage)(), 0, keepdims=False)

    def along(array, k):
        return lax.ppermute(array, "z", [(i, i ^ k) for i in range(chips)])

    first, second = pick(0), pick(1)
    first, second, queries = lax.optimization_barrier((first, second, queries))
    q_do = join_queries(queries)[:, None]
    q_do = lax.all_to_all(q_do, "core", 0, 1, tiled=True)
    far = range(chips - 1, 0, -1)
    one = {k: along(first, k) for k in far}
    two = {k: along(second[1], k) for k in far}
    over = lax.ppermute(
        jnp.stack([one[k][0] for k in far]), "pair", [(0, 1), (1, 0)]
    )

    def block(k):
        return lambda: 2 * lax.bitwise_xor(lax.axis_index("z"), k)

    stages = [
        (
            [first] + [one[k] for k in far],
            [(2, block(0), (0, (0,)), (0, (1,)))]
            + [(2, block(k), (i + 1, (0,)), (i + 1, (1,))) for i, k in enumerate(far)],
        ),
        (
            [second] + [two[k] for k in far] + [over],
            [(2, block(0), (0, (0,)), (0, (1,)))]
            + [(2, block(k), (chips, (i,)), (i + 1, ())) for i, k in enumerate(far)],
        ),
    ]
    dqs = []
    sums = []
    others = []
    for stage, (arrays, pieces) in enumerate(stages):
        *dq, dkv = attention(
            order,
            lengths,
            q_do,
            head_of(stage),
            arrays,
            pieces,
            parts,
            2,
            half,
            full,
            pieces[0][1],
            side,
            lambda: (lax.axis_index("head"), lax.axis_index("core")),
        )
        dkv = dkv.reshape((chips * parts * 2,) + dkv.shape[3:])
        dkv = lax.all_to_all(dkv, ("z", "head", "core"), 0, 0, tiled=True)
        if others:
            dkv, others[0] = lax.optimization_barrier((dkv, others[0]))
        dkv = dkv.reshape((chips, parts * 2) + dkv.shape[1:]).astype(F32)
        sums.append(jnp.sum(dkv, axis=0).astype(BF16))
        others.append(lax.ppermute(sums[stage][:, :, 0], "pair", [(0, 1), (1, 0)]))
        moved = dq[:1]
        for k in range(1, 4):
            to = 2 * (k % 2) + k // 2
            moved.append(
                lax.ppermute(dq[k], ("core", "head"), [(i, i ^ to) for i in range(4)])
            )
        dqs.append(moved)
    cut = rows * half // 2
    part = rows // parts
    straight = pair == 0

    def ordered(one, two, axis):
        return jnp.stack(
            [jnp.where(straight, one, two), jnp.where(straight, two, one)], axis=axis
        )

    index = 2 * lax.axis_index("head") + core

    def sorted_by_source(moved):
        a, b, c, d = [jnp.where(core == 0, moved[i], moved[i ^ 1]) for i in range(4)]
        low = index < 2
        return jnp.stack(
            [jnp.where(low, a, c), jnp.where(low, b, d), jnp.where(low, c, a), jnp.where(low, d, b)]
        )

    dqs = [sorted_by_source(moved) for moved in dqs]
    pref = ordered(*[d[:, :cut].reshape(-1, part, half, size) for d in dqs], 1)
    resp = ordered(*[d[:, cut:].reshape(-1, part, full, size) for d in dqs], 1)
    dq_pref = pref.transpose(2, 0, 1, 3, 4).reshape(part, -1, half, size)
    dq_resp = resp.transpose(2, 0, 1, 3, 4).reshape(part, -1, full, size)
    both = [
        (sums[i][:, :, 0].astype(F32) + others[1 - i].astype(F32)).astype(BF16) for i in range(2)
    ]
    pref = ordered(*both, 1)
    resp = ordered(*[s[:, :, 1] for s in sums], 1)
    pref = pref.transpose(2, 3, 0, 1, 4).reshape(2, part, -1, size)
    resp = resp.transpose(2, 3, 0, 1, 4).reshape(2, part, -1, size)
    return (dq_pref, pref[0], pref[1], dq_resp[None], resp[0][None], resp[1][None])


def gathered(key_value, queries, lengths, order, rows, half, full, size, side):
    q_do = join_queries(queries)
    parts = lax.axis_size("head")
    blk = ("z", "core")
    cores = lax.axis_size("core")
    heads = key_value.shape[0]
    part = rows // parts
    cut = rows * half // 2
    mine = lambda: lax.axis_index("z") * cores + lax.axis_index("core")
    pref_q, resp_q, pref_kv, resp_kv = [], [], [], []

    def exchange(array):
        return lax.all_to_all(array, "head", 0, 0, tiled=True)

    for g in range(heads):
        kv = lax.all_gather(key_value[g], blk, axis=1)
        *dq, dkv = attention(
            order,
            lengths,
            q_do[:, None],
            lambda g=g: g,
            [kv],
            [(kv.shape[1], lambda: 0, (0, (0,)), (0, (1,)))],
            1,
            1,
            half,
            full,
            mine,
            side,
            lambda: (0, 0),
        )
        dq = jnp.stack(dq)
        dkv = lax.psum_scatter(dkv, blk, scatter_dimension=0, tiled=True)
        dkv = dkv.reshape(2, 2, rows, size)
        own = lax.psum(dkv[:, 0].astype(F32), "pair").astype(BF16)
        pref_q.append(exchange(dq[:, :cut].reshape(parts, part, half, size)))
        resp_q.append(exchange(dq[:, cut:].reshape(parts, part, full, size)))
        pref_kv.append(exchange(own.reshape(2, parts, part, size).transpose(1, 0, 2, 3)))
        resp_kv.append(exchange(dkv[:, 1].reshape(2, parts, part, size).transpose(1, 0, 2, 3)))
    dq_pref = jnp.stack(pref_q, 1).transpose(2, 0, 1, 3, 4).reshape(part, -1, half, size)
    dq_resp = jnp.stack(resp_q, 1).transpose(2, 0, 1, 3, 4).reshape(part, -1, full, size)
    pref = jnp.stack(pref_kv, 1).transpose(2, 3, 0, 1, 4).reshape(2, part, -1, size)
    resp = jnp.stack(resp_kv, 1).transpose(2, 3, 0, 1, 4).reshape(2, part, -1, size)
    return (dq_pref, pref[0], pref[1], dq_resp[None], resp[0][None], resp[1][None])


def swap(local_heads, sizes):
    chips = sizes["blk"] // 2
    return local_heads == 4 and sizes["head"] == 2 and chips & (chips - 1) == 0


def solution(mesh):
    sizes = mesh.shape
    fine = Mesh(
        mesh.devices.reshape(sizes["blk"] // 2, 2, sizes["pair"], sizes["head"]),
        ("z", "core", "pair", "head"),
    )
    blk = ("z", "core")
    in_specs = (
        P(blk, "head", "pair", None),
        P(blk, "head", None),
        P(blk, "head", None),
        P(blk, "head", "pair", None),
        P("pair", blk, "head", None, None),
        P("pair", blk, "head", None),
        P("pair", blk, "head", None),
        P("pair", blk, "head", None, None),
        P(),
        P(),
    )
    rows = ("z", "core", "head")
    out_specs = (
        P(rows, None, "pair", None),
        P(rows, None, None),
        P(rows, None, None),
        P("pair", rows, None, None, None),
        P("pair", rows, None, None),
        P("pair", rows, None, None),
    )

    def run(*args):
        local_heads = args[1].shape[1] // sizes["head"]
        body = functools.partial(on_device, swap=swap(local_heads, sizes))
        step = jax.shard_map(
            body, mesh=fine, in_specs=in_specs, out_specs=out_specs, check_vma=False
        )
        return step(*args)

    return run
```

```python
import functools
import math

import jax
import jax.numpy as jnp
from jax import lax
from jax.experimental import pallas as pl
from jax.experimental.pallas import tpu as pltpu
from jax.sharding import Mesh, PartitionSpec as P

F32 = jnp.float32
BF16 = jnp.bfloat16
very_low = -1e30


def dot_nt(a, b):
    return lax.dot_general(a, b, (((1,), (1,)), ((), ())), preferred_element_type=F32)


def dot_nn(a, b):
    return lax.dot_general(a, b, (((1,), (0,)), ((), ())), preferred_element_type=F32)


def dot_tn(a, b):
    return lax.dot_general(a, b, (((0,), (0,)), ((), ())), preferred_element_type=F32)


def attn_kernel(
    order,
    lengths,
    *refs,
    pieces,
    inputs,
    slots,
    rows,
    half,
    full,
    first_block,
    side,
    flip,
):
    q_ref, do_ref = refs[:2]
    kv_refs = refs[2 : 2 + inputs]
    dq_refs = refs[2 + inputs : 2 + inputs + 2 * slots]
    dkv_ref, k_sc, v_sc, dk_sc, dv_sc, e_sc, p_sc, dq_sc = refs[2 + inputs + 2 * slots :]
    step = pl.program_id(0)
    head_size = q_ref.shape[-1]
    scaling = head_size**-0.5
    cexp = scaling * math.log2(math.e)
    total = k_sc.shape[0] // 2
    blocks = total // rows
    cut = rows * half

    @pl.when(step == 0)
    def _():
        for count, first, pref, resp in pieces:
            for i in range(count):
                j = first() + i
                for kind, at in ((pref, order[j] * rows), (resp, total + j * rows)):
                    array, lead = kind
                    at = pl.multiple_of(at, rows)
                    k_sc[pl.ds(at, rows), :] = kv_refs[array][lead + (i, 0)]
                    v_sc[pl.ds(at, rows), :] = kv_refs[array][lead + (i, 1)]
        dk_sc[...] = jnp.zeros_like(dk_sc)
        dv_sc[...] = jnp.zeros_like(dv_sc)

    def run(q, do, query_pos, chunks):
        tile = q.shape[0]
        parts = []
        for base, size, free in chunks:
            s = dot_nt(k_sc[base : base + size, :], q) * cexp
            if free < size:
                kp = base + free + lax.broadcasted_iota(jnp.int32, (size - free, tile), 0)
                tail = jnp.where(kp <= query_pos, s[free:], very_low)
                s = jnp.concatenate([s[:free], tail], axis=0) if free else tail
            dp = dot_nt(v_sc[base : base + size, :], do)
            m = jnp.max(s, axis=0, keepdims=True)
            e = jnp.exp2(s - m)
            e_sc[base : base + size, :tile] = e
            p_sc[base : base + size, :tile] = dp
            parts.append(
                (m, jnp.sum(e, axis=0, keepdims=True), jnp.sum(e * dp, axis=0, keepdims=True))
            )
        top = parts[0][0]
        for m, _, _ in parts[1:]:
            top = jnp.maximum(top, m)
        factors = [jnp.exp2(m - top) for m, _, _ in parts]
        inv = 1.0 / sum(f * l for f, (_, l, _) in zip(factors, parts))
        delta = sum(f * d for f, (_, _, d) in zip(factors, parts)) * inv
        acc = 0.0
        for f, (base, size, _) in zip(factors, chunks):
            p = e_sc[base : base + size, :tile] * (f * inv)
            ds = (p * (p_sc[base : base + size, :tile] - delta)).astype(BF16)
            dk_sc[base : base + size, :] += dot_nn(ds, q)
            dv_sc[base : base + size, :] += dot_nn(p.astype(BF16), do)
            acc = acc + dot_tn(k_sc[base : base + size, :], ds)
        return (acc * scaling).T.astype(BF16)

    @pl.when(step == 0)
    def _():
        def rows_of(ref):
            return jnp.concatenate([ref[0, i, 0, :cut] for i in range(slots)], axis=0)

        row = lax.broadcasted_iota(jnp.int32, (1, slots * cut), 1)
        offset = lax.shift_right_logical(row, int(math.log2(half)))
        pos = offset + order[first_block()] * rows
        for i in range(1, slots):
            here = offset - i * rows + order[first_block() + i] * rows
            pos = jnp.where(row < i * cut, pos, here)
        dq = run(rows_of(q_ref), rows_of(do_ref), pos, [(0, total, 0)])
        dq_sc[: slots * cut, :] = dq
        for index, ref in enumerate(dq_refs):
            at = (index % slots ^ flip()[1]) * cut + (index // slots ^ flip()[0]) * (cut // 2)
            ref[: cut // 2, :] = dq_sc[pl.ds(pl.multiple_of(at, cut // 2), cut // 2), :]

    @pl.when(step > 0)
    def _():
        slot = step - 1
        block = first_block() + slot
        tile = rows * full
        live = block * rows < lengths[side()]

        @pl.when(live)
        def _():
            row = lax.broadcasted_iota(jnp.int32, (1, tile), 1)
            pos = total + block * rows + lax.shift_right_logical(row, int(math.log2(full)))
            if 2 * total <= 2048:
                chunks = [(0, 2 * total, total)]
            else:
                chunks = [(at, 1024, 1024 if at < total else 0) for at in range(0, 2 * total, 1024)]
            dq_sc[:tile, :] = run(
                q_ref[0, slot, 0, pl.ds(cut, tile)], do_ref[0, slot, 0, pl.ds(cut, tile)], pos, chunks
            )

        @pl.when(jnp.logical_not(live))
        def _():
            dq_sc[:tile, :] = jnp.zeros((tile, head_size), BF16)

        for index, ref in enumerate(dq_refs):

            @pl.when(slot == index % slots ^ flip()[1])
            def _(index=index, ref=ref):
                at = (index // slots ^ flip()[0]) * (tile // 2)
                ref[cut // 2 :, :] = dq_sc[pl.ds(pl.multiple_of(at, tile // 2), tile // 2), :]

    @pl.when(step == slots)
    def _():
        parts, group = dkv_ref.shape[1:3]
        rows_out = rows // parts
        for j in range(blocks):
            for h in range(parts):
                at = pl.multiple_of(order[j] * rows + h * rows_out, rows_out)
                out = dkv_ref.at[j // group, h, j % group]
                out[0, 0] = (dk_sc[pl.ds(at, rows_out), :] * scaling).astype(BF16)
                out[1, 0] = dv_sc[pl.ds(at, rows_out), :].astype(BF16)
                at = total + j * rows + h * rows_out
                out[0, 1] = (dk_sc[pl.ds(at, rows_out), :] * scaling).astype(BF16)
                out[1, 1] = dv_sc[pl.ds(at, rows_out), :].astype(BF16)


def whole(shape):
    return pl.BlockSpec(shape, lambda *_: (0,) * len(shape))


def attention(order, lengths, q_do, head, arrays, pieces, parts, group, half, full, first_block, side, flip):
    slots = q_do.shape[1]
    size = q_do.shape[-1]
    rows = arrays[0].shape[-2]
    blocks = order.shape[0]
    tile = rows * max(slots * half, full)
    keys = 2 * blocks * rows
    kern = functools.partial(
        attn_kernel,
        pieces=pieces,
        inputs=len(arrays),
        slots=slots,
        rows=rows,
        half=half,
        full=full,
        first_block=first_block,
        side=side,
        flip=flip,
    )
    out_rows = rows // 2 * (half + full)
    dkv_shape = (blocks // group, parts, group, 2, 2, rows // parts, size)

    def q_spec(which):
        return pl.BlockSpec(
            (1, slots, 1, rows * (half + full), size), lambda t, *_: (head(), 0, which, 0, 0)
        )

    spec = pltpu.PrefetchScalarGridSpec(
        num_scalar_prefetch=2,
        grid=(1 + slots,),
        in_specs=[q_spec(0), q_spec(1)] + [whole(a.shape) for a in arrays],
        out_specs=[whole((out_rows, size))] * (2 * slots) + [whole(dkv_shape)],
        scratch_shapes=[
            pltpu.VMEM((keys, size), BF16),
            pltpu.VMEM((keys, size), BF16),
            pltpu.VMEM((keys, size), F32),
            pltpu.VMEM((keys, size), F32),
            pltpu.VMEM((keys, tile), F32),
            pltpu.VMEM((keys, tile), F32),
            pltpu.VMEM((tile, size), BF16),
        ],
    )
    work = slots * rows * (full + half // 2) * keys
    return pl.pallas_call(
        kern,
        grid_spec=spec,
        out_shape=[jax.ShapeDtypeStruct((out_rows, size), BF16)] * (2 * slots)
        + [jax.ShapeDtypeStruct(dkv_shape, BF16)],
        compiler_params=pltpu.CompilerParams(vmem_limit_bytes=62 << 20),
        cost_estimate=pl.CostEstimate(
            flops=10 * work * size, bytes_accessed=16 << 20, transcendentals=work
        ),
    )(order, lengths, q_do, q_do, *arrays)


def split_heads(array):
    rows, heads, group, size = array.shape
    return array.transpose(1, 0, 2, 3).reshape(heads, rows * group, size)


def on_device(
    prefix_query_rows,
    prefix_key_rows,
    prefix_value_rows,
    prefix_output_gradient,
    resp_q,
    resp_k,
    response_value_rows,
    response_output_gradient,
    lengths,
    prefix_order,
    *,
    swap,
):
    rows, local_heads, half, size = prefix_query_rows.shape
    full = resp_q.shape[3]
    key_value = jnp.stack(
        [prefix_key_rows, prefix_value_rows, resp_k[0], response_value_rows[0]]
    ).reshape(2, 2, rows, local_heads, size)
    key_value = key_value.transpose(3, 0, 1, 2, 4)
    queries = (
        prefix_query_rows,
        resp_q[0],
        prefix_output_gradient,
        response_output_gradient[0],
    )
    side = lambda: lax.axis_index("pair")
    work = swapped if swap else gathered
    return work(key_value, queries, lengths, prefix_order, rows, half, full, size, side)


def join_queries(queries):
    parts = [split_heads(a) for a in queries]
    return jnp.stack(
        [jnp.concatenate(parts[:2], axis=1), jnp.concatenate(parts[2:], axis=1)], axis=1
    )


def assemble_kernel(*refs, cut, half):
    pieces, pref_ref, resp_ref = (refs[:4], refs[4:8]), refs[8], refs[9]
    head, core, pair = [lax.axis_index(name) for name in ("head", "core", "pair")]
    for k in range(4):
        source = 2 * (head ^ (k // 2)) + (core ^ (k % 2))
        for stage in range(2):
            resp_ref[:, 2 * source + (pair ^ stage)] = pieces[stage][k][cut:]
        zero, one = [p[k][:cut].astype(F32) for p in pieces]
        first = jnp.where(pair == 0, zero, one)
        second = jnp.where(pair == 0, one, zero)
        low = lax.broadcasted_iota(jnp.int32, first.shape, 1) < half
        even = jnp.where(low, first, pltpu.roll(second, half, 1))
        odd = jnp.where(low, pltpu.roll(first, half, 1), second)
        pref_ref[:, source] = jnp.stack([even, odd], 1).reshape(pref_ref[:, source].shape).astype(BF16)


def assemble(dqs, part, half, full, size):
    group = 2 * half
    pieces = [a.reshape(-1, group, size) for moved in dqs for a in moved]
    pref, resp = pl.pallas_call(
        functools.partial(assemble_kernel, cut=part * half // group, half=half),
        out_shape=[
            jax.ShapeDtypeStruct((part, 4, group, size), BF16),
            jax.ShapeDtypeStruct((part, 8, full, size), BF16),
        ],
        compiler_params=pltpu.CompilerParams(vmem_limit_bytes=12 << 20),
        cost_estimate=pl.CostEstimate(flops=0, bytes_accessed=3 << 20, transcendentals=0),
    )(*pieces)
    return pref.reshape(part, 8, half, size), resp


def swapped(key_value, queries, lengths, order, rows, half, full, size, side):
    chips = lax.axis_size("z")
    parts = lax.axis_size("head")
    heads = key_value.shape[0] // 2
    core = lax.axis_index("core")
    pair = lax.axis_index("pair")
    keep = lax.dynamic_slice_in_dim(key_value, core * heads, heads, 0)
    give = lax.dynamic_slice_in_dim(key_value, (1 - core) * heads, heads, 0)
    take = lax.ppermute(give, "core", [(0, 1), (1, 0)])
    mine = core == 0
    key_value = jnp.stack([jnp.where(mine, keep, take), jnp.where(mine, take, keep)], axis=2)

    def head_of(stage):
        return lambda: lax.bitwise_xor(lax.axis_index("pair"), stage)

    def pick(stage):
        return lax.dynamic_index_in_dim(key_value, head_of(stage)(), 0, keepdims=False)

    def along(array, k):
        return lax.ppermute(array, "z", [(i, i ^ k) for i in range(chips)])

    first, second = pick(0), pick(1)
    first, second, queries = lax.optimization_barrier((first, second, queries))
    q_do = join_queries(queries)[:, None]
    q_do = lax.all_to_all(q_do, "core", 0, 1, tiled=True)
    far = range(chips - 1, 0, -1)
    one = {k: along(first, k) for k in far}
    two = {k: along(second[1], k) for k in far}
    over = lax.ppermute(
        jnp.stack([one[k][0] for k in far]), "pair", [(0, 1), (1, 0)]
    )

    def block(k):
        return lambda: 2 * lax.bitwise_xor(lax.axis_index("z"), k)

    stages = [
        (
            [first] + [one[k] for k in far],
            [(2, block(0), (0, (0,)), (0, (1,)))]
            + [(2, block(k), (i + 1, (0,)), (i + 1, (1,))) for i, k in enumerate(far)],
        ),
        (
            [second] + [two[k] for k in far] + [over],
            [(2, block(0), (0, (0,)), (0, (1,)))]
            + [(2, block(k), (chips, (i,)), (i + 1, ())) for i, k in enumerate(far)],
        ),
    ]
    dqs = []
    sums = []
    others = []
    for stage, (arrays, pieces) in enumerate(stages):
        *dq, dkv = attention(
            order,
            lengths,
            q_do,
            head_of(stage),
            arrays,
            pieces,
            parts,
            2,
            half,
            full,
            pieces[0][1],
            side,
            lambda: (lax.axis_index("head"), lax.axis_index("core")),
        )
        dkv = dkv.reshape((chips * parts * 2,) + dkv.shape[3:])
        dkv = lax.all_to_all(dkv, ("z", "head", "core"), 0, 0, tiled=True)
        if others:
            dkv, others[0] = lax.optimization_barrier((dkv, others[0]))
        dkv = dkv.reshape((chips, parts * 2) + dkv.shape[1:]).astype(F32)
        sums.append(jnp.sum(dkv, axis=0).astype(BF16))
        others.append(lax.ppermute(sums[stage][:, :, 0], "pair", [(0, 1), (1, 0)]))
        moved = dq[:1]
        for k in range(1, 4):
            to = 2 * (k % 2) + k // 2
            moved.append(
                lax.ppermute(dq[k], ("core", "head"), [(i, i ^ to) for i in range(4)])
            )
        dqs.append(moved)
    part = rows // parts
    straight = pair == 0

    def ordered(one, two, axis):
        return jnp.stack(
            [jnp.where(straight, one, two), jnp.where(straight, two, one)], axis=axis
        )

    dq_pref, dq_resp = assemble(dqs, part, half, full, size)
    both = [
        (sums[i][:, :, 0].astype(F32) + others[1 - i].astype(F32)).astype(BF16) for i in range(2)
    ]
    pref = ordered(*both, 1)
    resp = ordered(*[s[:, :, 1] for s in sums], 1)
    pref = pref.transpose(2, 3, 0, 1, 4).reshape(2, part, -1, size)
    resp = resp.transpose(2, 3, 0, 1, 4).reshape(2, part, -1, size)
    return (dq_pref, pref[0], pref[1], dq_resp[None], resp[0][None], resp[1][None])


def gathered(key_value, queries, lengths, order, rows, half, full, size, side):
    q_do = join_queries(queries)
    parts = lax.axis_size("head")
    blk = ("z", "core")
    cores = lax.axis_size("core")
    heads = key_value.shape[0]
    part = rows // parts
    cut = rows * half // 2
    mine = lambda: lax.axis_index("z") * cores + lax.axis_index("core")
    pref_q, resp_q, pref_kv, resp_kv = [], [], [], []

    def exchange(array):
        return lax.all_to_all(array, "head", 0, 0, tiled=True)

    for g in range(heads):
        kv = lax.all_gather(key_value[g], blk, axis=1)
        *dq, dkv = attention(
            order,
            lengths,
            q_do[:, None],
            lambda g=g: g,
            [kv],
            [(kv.shape[1], lambda: 0, (0, (0,)), (0, (1,)))],
            1,
            1,
            half,
            full,
            mine,
            side,
            lambda: (0, 0),
        )
        dq = jnp.stack(dq)
        dkv = lax.psum_scatter(dkv, blk, scatter_dimension=0, tiled=True)
        dkv = dkv.reshape(2, 2, rows, size)
        own = lax.psum(dkv[:, 0].astype(F32), "pair").astype(BF16)
        pref_q.append(exchange(dq[:, :cut].reshape(parts, part, half, size)))
        resp_q.append(exchange(dq[:, cut:].reshape(parts, part, full, size)))
        pref_kv.append(exchange(own.reshape(2, parts, part, size).transpose(1, 0, 2, 3)))
        resp_kv.append(exchange(dkv[:, 1].reshape(2, parts, part, size).transpose(1, 0, 2, 3)))
    dq_pref = jnp.stack(pref_q, 1).transpose(2, 0, 1, 3, 4).reshape(part, -1, half, size)
    dq_resp = jnp.stack(resp_q, 1).transpose(2, 0, 1, 3, 4).reshape(part, -1, full, size)
    pref = jnp.stack(pref_kv, 1).transpose(2, 3, 0, 1, 4).reshape(2, part, -1, size)
    resp = jnp.stack(resp_kv, 1).transpose(2, 3, 0, 1, 4).reshape(2, part, -1, size)
    return (dq_pref, pref[0], pref[1], dq_resp[None], resp[0][None], resp[1][None])


def swap(local_heads, sizes, half, full):
    chips = sizes["blk"] // 2
    shapes = (local_heads, sizes["head"], half, full) == (4, 2, 4, 8)
    return shapes and chips & (chips - 1) == 0


def solution(mesh):
    sizes = mesh.shape
    fine = Mesh(
        mesh.devices.reshape(sizes["blk"] // 2, 2, sizes["pair"], sizes["head"]),
        ("z", "core", "pair", "head"),
    )
    blk = ("z", "core")
    in_specs = (
        P(blk, "head", "pair", None),
        P(blk, "head", None),
        P(blk, "head", None),
        P(blk, "head", "pair", None),
        P("pair", blk, "head", None, None),
        P("pair", blk, "head", None),
        P("pair", blk, "head", None),
        P("pair", blk, "head", None, None),
        P(),
        P(),
    )
    rows = ("z", "core", "head")
    out_specs = (
        P(rows, None, "pair", None),
        P(rows, None, None),
        P(rows, None, None),
        P("pair", rows, None, None, None),
        P("pair", rows, None, None),
        P("pair", rows, None, None),
    )

    def run(*args):
        local_heads = args[1].shape[1] // sizes["head"]
        body = functools.partial(on_device, swap=swap(local_heads, sizes, args[0].shape[2] // sizes["pair"], args[4].shape[3]))
        step = jax.shard_map(
            body, mesh=fine, in_specs=in_specs, out_specs=out_specs, check_vma=False
        )
        return step(*args)

    return run
```

```python
import functools
import math

import jax
import jax.numpy as jnp
from jax import lax
from jax.experimental import pallas as pl
from jax.experimental.pallas import tpu as pltpu
from jax.sharding import Mesh, PartitionSpec as P

F32 = jnp.float32
BF16 = jnp.bfloat16
very_low = -1e30


def dot_nt(a, b):
    return lax.dot_general(a, b, (((1,), (1,)), ((), ())), preferred_element_type=F32)


def dot_nn(a, b):
    return lax.dot_general(a, b, (((1,), (0,)), ((), ())), preferred_element_type=F32)


def dot_tn(a, b):
    return lax.dot_general(a, b, (((0,), (0,)), ((), ())), preferred_element_type=F32)


def attn_kernel(
    order,
    lengths,
    *refs,
    pieces,
    inputs,
    slots,
    rows,
    half,
    full,
    first_block,
    side,
    flip,
    mode,
):
    refs = list(refs)

    def take(count):
        got = refs[:count]
        del refs[:count]
        return got

    q_ref, do_ref = take(2)
    kv_refs = take(inputs)
    dq_in, carried = (take(2 * slots), take(2)) if mode == "pref" else ([], [])
    dq_refs = take(2 * slots)
    outs = take(1 if mode != "resp" else len(pieces) + 2)
    k_sc, v_sc, dk_sc, dv_sc, e_sc, p_sc, dq_sc = refs
    step = pl.program_id(0)
    head_size = q_ref.shape[-1]
    scaling = head_size**-0.5
    cexp = scaling * math.log2(math.e)
    total = k_sc.shape[0] // 2
    blocks = total // rows
    cut = rows * half

    @pl.when(step == 0)
    def _():
        for count, first, pref, resp in pieces:
            for i in range(count):
                j = first() + i
                kinds = [(pref, order[j] * rows), (resp, total + j * rows)]
                for kind, at in kinds[: 1 if mode == "pref" else 2]:
                    array, lead = kind
                    at = pl.multiple_of(at, rows)
                    k_sc[pl.ds(at, rows), :] = kv_refs[array][lead + (i, 0)]
                    v_sc[pl.ds(at, rows), :] = kv_refs[array][lead + (i, 1)]
        if carried:
            dk_sc[:total, :] = carried[0][...]
            dv_sc[:total, :] = carried[1][...]
        else:
            dk_sc[...] = jnp.zeros_like(dk_sc)
            dv_sc[...] = jnp.zeros_like(dv_sc)

    def run(q, do, query_pos, chunks):
        tile = q.shape[0]
        parts = []
        for base, size, free in chunks:
            s = dot_nt(k_sc[base : base + size, :], q) * cexp
            if free < size:
                kp = base + free + lax.broadcasted_iota(jnp.int32, (size - free, tile), 0)
                tail = jnp.where(kp <= query_pos, s[free:], very_low)
                s = jnp.concatenate([s[:free], tail], axis=0) if free else tail
            dp = dot_nt(v_sc[base : base + size, :], do)
            m = jnp.max(s, axis=0, keepdims=True)
            e = jnp.exp2(s - m)
            e_sc[base : base + size, :tile] = e
            p_sc[base : base + size, :tile] = dp
            parts.append(
                (m, jnp.sum(e, axis=0, keepdims=True), jnp.sum(e * dp, axis=0, keepdims=True))
            )
        top = parts[0][0]
        for m, _, _ in parts[1:]:
            top = jnp.maximum(top, m)
        factors = [jnp.exp2(m - top) for m, _, _ in parts]
        inv = 1.0 / sum(f * l for f, (_, l, _) in zip(factors, parts))
        delta = sum(f * d for f, (_, _, d) in zip(factors, parts)) * inv
        acc = 0.0
        for f, (base, size, _) in zip(factors, chunks):
            p = e_sc[base : base + size, :tile] * (f * inv)
            ds = (p * (p_sc[base : base + size, :tile] - delta)).astype(BF16)
            dk_sc[base : base + size, :] += dot_nn(ds, q)
            dv_sc[base : base + size, :] += dot_nn(p.astype(BF16), do)
            acc = acc + dot_tn(k_sc[base : base + size, :], ds)
        return (acc * scaling).T.astype(BF16)

    def prefix_step():
        def rows_of(ref):
            return jnp.concatenate([ref[0, i, 0, :cut] for i in range(slots)], axis=0)

        row = lax.broadcasted_iota(jnp.int32, (1, slots * cut), 1)
        offset = lax.shift_right_logical(row, int(math.log2(half)))
        pos = offset + order[first_block()] * rows
        for i in range(1, slots):
            here = offset - i * rows + order[first_block() + i] * rows
            pos = jnp.where(row < i * cut, pos, here)
        dq = run(rows_of(q_ref), rows_of(do_ref), pos, [(0, total, 0)])
        dq_sc[: slots * cut, :] = dq
        for index, ref in enumerate(dq_refs):
            at = (index % slots ^ flip()[1]) * cut + (index // slots ^ flip()[0]) * (cut // 2)
            ref[: cut // 2, :] = dq_sc[pl.ds(pl.multiple_of(at, cut // 2), cut // 2), :]
            if dq_in:
                ref[cut // 2 :, :] = dq_in[index][...]

    def response_step():
        slot = step - before
        block = first_block() + slot
        tile = rows * full
        live = block * rows < lengths[side()]

        @pl.when(live)
        def _():
            row = lax.broadcasted_iota(jnp.int32, (1, tile), 1)
            pos = total + block * rows + lax.shift_right_logical(row, int(math.log2(full)))
            if 2 * total <= 2048:
                chunks = [(0, 2 * total, total)]
            else:
                chunks = [(at, 1024, 1024 if at < total else 0) for at in range(0, 2 * total, 1024)]
            dq_sc[:tile, :] = run(
                q_ref[0, slot, 0, pl.ds(cut, tile)], do_ref[0, slot, 0, pl.ds(cut, tile)], pos, chunks
            )

        @pl.when(jnp.logical_not(live))
        def _():
            dq_sc[:tile, :] = jnp.zeros((tile, head_size), BF16)

        for index, ref in enumerate(dq_refs):

            @pl.when(slot == index % slots ^ flip()[1])
            def _(index=index, ref=ref):
                at = (index // slots ^ flip()[0]) * (tile // 2)
                got = dq_sc[pl.ds(pl.multiple_of(at, tile // 2), tile // 2), :]
                ref[ref.shape[0] - tile // 2 :, :] = got

    before = 0 if mode == "resp" else 1
    if mode != "resp":
        pl.when(step == 0)(prefix_step)
    if mode != "pref":
        pl.when(step >= before)(response_step)

    def grads_at(at, count):
        at = pl.multiple_of(at, count)
        dk = (dk_sc[pl.ds(at, count), :] * scaling).astype(BF16)
        return dk, dv_sc[pl.ds(at, count), :].astype(BF16)

    @pl.when(step == pl.num_programs(0) - 1)
    def _():
        if mode == "resp":
            rows_out = rows // 2
            for k, out in enumerate(outs[:-2]):
                for index in range(2 * slots):
                    block = pieces[k][1]() + (index % slots ^ flip()[1])
                    at = total + block * rows + (index // slots ^ flip()[0]) * rows_out
                    out[index, 0], out[index, 1] = grads_at(at, rows_out)
            outs[-2][...] = dk_sc[:total, :]
            outs[-1][...] = dv_sc[:total, :]
            return
        parts, group = outs[0].shape[1:3]
        rows_out = rows // parts
        for j in range(blocks):
            for h in range(parts):
                out = outs[0].at[j // group, h, j % group]
                got = grads_at(order[j] * rows + h * rows_out, rows_out)
                out[0, 0], out[1, 0] = got
                if mode == "both":
                    got = grads_at(total + j * rows + h * rows_out, rows_out)
                    out[0, 1], out[1, 1] = got


def whole(shape):
    return pl.BlockSpec(shape, lambda *_: (0,) * len(shape))


def attention(order, lengths, q_do, head, arrays, pieces, parts, group, half, full, first_block, side, flip, mode="both", carried=()):
    slots = q_do.shape[1]
    size = q_do.shape[-1]
    rows = arrays[0].shape[-2]
    blocks = order.shape[0]
    tile = rows * max(slots * half, full)
    keys = 2 * blocks * rows
    kern = functools.partial(
        attn_kernel,
        pieces=pieces,
        inputs=len(arrays),
        slots=slots,
        rows=rows,
        half=half,
        full=full,
        first_block=first_block,
        side=side,
        flip=flip,
        mode=mode,
    )
    out_rows = rows // 2 * {"both": half + full, "resp": full, "pref": half + full}[mode]
    kinds = 2 if mode == "both" else 1
    outs = [jax.ShapeDtypeStruct((out_rows, size), BF16)] * (2 * slots)
    if mode == "resp":
        outs += [jax.ShapeDtypeStruct((2 * slots, 2, rows // 2, size), BF16)] * len(pieces)
        outs += [jax.ShapeDtypeStruct((blocks * rows, size), F32)] * 2
    else:
        shape = (blocks // group, parts, group, 2, kinds, rows // parts, size)
        outs += [jax.ShapeDtypeStruct(shape, BF16)]
    q_rows = rows * (half if mode == "pref" else half + full)
    steps = {"both": 1 + slots, "resp": slots, "pref": 1}[mode]

    def q_spec(which):
        return pl.BlockSpec(
            (1, slots, 1, q_rows, size), lambda t, *_: (head(), 0, which, 0, 0)
        )

    spec = pltpu.PrefetchScalarGridSpec(
        num_scalar_prefetch=2,
        grid=(steps,),
        in_specs=[q_spec(0), q_spec(1)] + [whole(a.shape) for a in list(arrays) + list(carried)],
        out_specs=[whole(a.shape) for a in outs],
        scratch_shapes=[
            pltpu.VMEM((keys, size), BF16),
            pltpu.VMEM((keys, size), BF16),
            pltpu.VMEM((keys, size), F32),
            pltpu.VMEM((keys, size), F32),
            pltpu.VMEM((keys, tile), F32),
            pltpu.VMEM((keys, tile), F32),
            pltpu.VMEM((tile, size), BF16),
        ],
    )
    work = slots * rows * (full + half // 2) * keys
    return pl.pallas_call(
        kern,
        grid_spec=spec,
        out_shape=outs,
        compiler_params=pltpu.CompilerParams(vmem_limit_bytes=62 << 20),
        cost_estimate=pl.CostEstimate(
            flops=10 * work * size, bytes_accessed=16 << 20, transcendentals=work
        ),
    )(order, lengths, q_do, q_do, *arrays, *carried)


def split_heads(array):
    rows, heads, group, size = array.shape
    return array.transpose(1, 0, 2, 3).reshape(heads, rows * group, size)


def on_device(
    prefix_query_rows,
    prefix_key_rows,
    prefix_value_rows,
    prefix_output_gradient,
    resp_q,
    resp_k,
    response_value_rows,
    response_output_gradient,
    lengths,
    prefix_order,
    *,
    swap,
):
    rows, local_heads, half, size = prefix_query_rows.shape
    full = resp_q.shape[3]
    key_value = jnp.stack(
        [prefix_key_rows, prefix_value_rows, resp_k[0], response_value_rows[0]]
    ).reshape(2, 2, rows, local_heads, size)
    key_value = key_value.transpose(3, 0, 1, 2, 4)
    queries = (
        prefix_query_rows,
        resp_q[0],
        prefix_output_gradient,
        response_output_gradient[0],
    )
    side = lambda: lax.axis_index("pair")
    work = swapped if swap else gathered
    return work(key_value, queries, lengths, prefix_order, rows, half, full, size, side)


def join_queries(queries):
    parts = [split_heads(a) for a in queries]
    return jnp.stack(
        [jnp.concatenate(parts[:2], axis=1), jnp.concatenate(parts[2:], axis=1)], axis=1
    )


def assemble_kernel(*refs, cut, half):
    pieces, pref_ref, resp_ref = (refs[:4], refs[4:8]), refs[8], refs[9]
    head, core, pair = [lax.axis_index(name) for name in ("head", "core", "pair")]
    for k in range(4):
        source = 2 * (head ^ (k // 2)) + (core ^ (k % 2))
        for stage in range(2):
            resp_ref[:, 2 * source + (pair ^ stage)] = pieces[stage][k][cut:]
        zero, one = [p[k][:cut].astype(F32) for p in pieces]
        first = jnp.where(pair == 0, zero, one)
        second = jnp.where(pair == 0, one, zero)
        low = lax.broadcasted_iota(jnp.int32, first.shape, 1) < half
        even = jnp.where(low, first, pltpu.roll(second, half, 1))
        odd = jnp.where(low, pltpu.roll(first, half, 1), second)
        pref_ref[:, source] = jnp.stack([even, odd], 1).reshape(pref_ref[:, source].shape).astype(BF16)


def assemble(dqs, part, half, full, size):
    group = 2 * half
    pieces = [a.reshape(-1, group, size) for moved in dqs for a in moved]
    pref, resp = pl.pallas_call(
        functools.partial(assemble_kernel, cut=part * half // group, half=half),
        out_shape=[
            jax.ShapeDtypeStruct((part, 4, group, size), BF16),
            jax.ShapeDtypeStruct((part, 8, full, size), BF16),
        ],
        compiler_params=pltpu.CompilerParams(vmem_limit_bytes=12 << 20),
        cost_estimate=pl.CostEstimate(flops=0, bytes_accessed=3 << 20, transcendentals=0),
    )(*pieces)
    return pref.reshape(part, 8, half, size), resp


def swapped(key_value, queries, lengths, order, rows, half, full, size, side):
    chips = lax.axis_size("z")
    parts = lax.axis_size("head")
    heads = key_value.shape[0] // 2
    core = lax.axis_index("core")
    pair = lax.axis_index("pair")
    keep = lax.dynamic_slice_in_dim(key_value, core * heads, heads, 0)
    give = lax.dynamic_slice_in_dim(key_value, (1 - core) * heads, heads, 0)
    take = lax.ppermute(give, "core", [(0, 1), (1, 0)])
    mine = core == 0
    key_value = jnp.stack([jnp.where(mine, keep, take), jnp.where(mine, take, keep)], axis=2)

    def head_of(stage):
        return lambda: lax.bitwise_xor(lax.axis_index("pair"), stage)

    def pick(stage):
        return lax.dynamic_index_in_dim(key_value, head_of(stage)(), 0, keepdims=False)

    def along(array, k):
        return lax.ppermute(array, "z", [(i, i ^ k) for i in range(chips)])

    first, second = pick(0), pick(1)
    first, second, queries = lax.optimization_barrier((first, second, queries))
    q_do = join_queries(queries)[:, None]
    q_do = lax.all_to_all(q_do, "core", 0, 1, tiled=True)
    far = range(chips - 1, 0, -1)
    one = {k: along(first, k) for k in far}
    two = {k: along(second[1], k) for k in far}
    over = lax.ppermute(
        jnp.stack([one[k][0] for k in far]), "pair", [(0, 1), (1, 0)]
    )

    def block(k):
        return lambda: 2 * lax.bitwise_xor(lax.axis_index("z"), k)

    stages = [
        (
            [first] + [one[k] for k in far],
            [(2, block(0), (0, (0,)), (0, (1,)))]
            + [(2, block(k), (i + 1, (0,)), (i + 1, (1,))) for i, k in enumerate(far)],
        ),
        (
            [second] + [two[k] for k in far] + [over],
            [(2, block(0), (0, (0,)), (0, (1,)))]
            + [(2, block(k), (chips, (i,)), (i + 1, ())) for i, k in enumerate(far)],
        ),
    ]
    dqs = []
    others = []
    flip = lambda: (lax.axis_index("head"), lax.axis_index("core"))

    def run(stage, arrays, pieces, mode, carried=()):
        return attention(
            order,
            lengths,
            q_do,
            head_of(stage),
            arrays,
            pieces,
            parts,
            2,
            half,
            full,
            block(0),
            side,
            flip,
            mode,
            carried,
        )

    def to_owners(dkv):
        dkv = dkv.reshape((chips * parts * 2,) + dkv.shape[3:])
        dkv = lax.all_to_all(dkv, ("z", "head", "core"), 0, 0, tiled=True)
        if others:
            dkv, others[0] = lax.optimization_barrier((dkv, others[0]))
        dkv = dkv.reshape((chips, parts * 2) + dkv.shape[1:]).astype(F32)
        return jnp.sum(dkv, axis=0).astype(BF16)

    def to_pair(array):
        others.append(lax.ppermute(array, "pair", [(0, 1), (1, 0)]))

    def around(arrays):
        moved = list(arrays[:1])
        for k in range(1, 4):
            to = 2 * (k % 2) + k // 2
            moved.append(lax.ppermute(arrays[k], ("core", "head"), [(i, i ^ to) for i in range(4)]))
        return moved

    *dq, dkv = run(0, *stages[0], "both")
    zero = to_owners(dkv)
    to_pair(zero[:, :, 0])
    dqs.append(around(dq))
    *got, carry_k, carry_v = run(1, *stages[1], "resp")
    dq, dr = got[:4], got[4:]
    dr = [dr[0]] + [along(a, k) for a, k in zip(dr[1:], far)]
    *dq, dkv = run(1, *stages[1], "pref", dq + [carry_k, carry_v])
    one_pref = to_owners(dkv)[:, :, 0]
    to_pair(one_pref)
    dqs.append(around(dq))
    dr = sum(a.astype(F32) for a in dr).astype(BF16)
    moved = around([dr[k] for k in range(4)])
    part = rows // parts
    straight = pair == 0

    def ordered(one, two, axis):
        return jnp.stack(
            [jnp.where(straight, one, two), jnp.where(straight, two, one)], axis=axis
        )

    dq_pref, dq_resp = assemble(dqs, part, half, full, size)
    low = lax.axis_index("head") == 0
    a, b, c, d = [jnp.where(core == 0, moved[i], moved[i ^ 1]) for i in range(4)]
    one_resp = jnp.stack(
        [jnp.where(low, a, c), jnp.where(low, b, d), jnp.where(low, c, a), jnp.where(low, d, b)]
    )
    pref = [
        (mine.astype(F32) + other.astype(F32)).astype(BF16)
        for mine, other in ((zero[:, :, 0], others[1]), (one_pref, others[0]))
    ]
    pref = ordered(*pref, 1)
    resp = ordered(zero[:, :, 1], one_resp, 1)
    pref = pref.transpose(2, 3, 0, 1, 4).reshape(2, part, -1, size)
    resp = resp.transpose(2, 3, 0, 1, 4).reshape(2, part, -1, size)
    return (dq_pref, pref[0], pref[1], dq_resp[None], resp[0][None], resp[1][None])


def gathered(key_value, queries, lengths, order, rows, half, full, size, side):
    q_do = join_queries(queries)
    parts = lax.axis_size("head")
    blk = ("z", "core")
    cores = lax.axis_size("core")
    heads = key_value.shape[0]
    part = rows // parts
    cut = rows * half // 2
    mine = lambda: lax.axis_index("z") * cores + lax.axis_index("core")
    pref_q, resp_q, pref_kv, resp_kv = [], [], [], []

    def exchange(array):
        return lax.all_to_all(array, "head", 0, 0, tiled=True)

    for g in range(heads):
        kv = lax.all_gather(key_value[g], blk, axis=1)
        *dq, dkv = attention(
            order,
            lengths,
            q_do[:, None],
            lambda g=g: g,
            [kv],
            [(kv.shape[1], lambda: 0, (0, (0,)), (0, (1,)))],
            1,
            1,
            half,
            full,
            mine,
            side,
            lambda: (0, 0),
        )
        dq = jnp.stack(dq)
        dkv = lax.psum_scatter(dkv, blk, scatter_dimension=0, tiled=True)
        dkv = dkv.reshape(2, 2, rows, size)
        own = lax.psum(dkv[:, 0].astype(F32), "pair").astype(BF16)
        pref_q.append(exchange(dq[:, :cut].reshape(parts, part, half, size)))
        resp_q.append(exchange(dq[:, cut:].reshape(parts, part, full, size)))
        pref_kv.append(exchange(own.reshape(2, parts, part, size).transpose(1, 0, 2, 3)))
        resp_kv.append(exchange(dkv[:, 1].reshape(2, parts, part, size).transpose(1, 0, 2, 3)))
    dq_pref = jnp.stack(pref_q, 1).transpose(2, 0, 1, 3, 4).reshape(part, -1, half, size)
    dq_resp = jnp.stack(resp_q, 1).transpose(2, 0, 1, 3, 4).reshape(part, -1, full, size)
    pref = jnp.stack(pref_kv, 1).transpose(2, 3, 0, 1, 4).reshape(2, part, -1, size)
    resp = jnp.stack(resp_kv, 1).transpose(2, 3, 0, 1, 4).reshape(2, part, -1, size)
    return (dq_pref, pref[0], pref[1], dq_resp[None], resp[0][None], resp[1][None])


def swap(local_heads, sizes, half, full):
    chips = sizes["blk"] // 2
    shapes = (local_heads, sizes["head"], half, full) == (4, 2, 4, 8)
    return shapes and chips & (chips - 1) == 0


def solution(mesh):
    sizes = mesh.shape
    fine = Mesh(
        mesh.devices.reshape(sizes["blk"] // 2, 2, sizes["pair"], sizes["head"]),
        ("z", "core", "pair", "head"),
    )
    blk = ("z", "core")
    in_specs = (
        P(blk, "head", "pair", None),
        P(blk, "head", None),
        P(blk, "head", None),
        P(blk, "head", "pair", None),
        P("pair", blk, "head", None, None),
        P("pair", blk, "head", None),
        P("pair", blk, "head", None),
        P("pair", blk, "head", None, None),
        P(),
        P(),
    )
    rows = ("z", "core", "head")
    out_specs = (
        P(rows, None, "pair", None),
        P(rows, None, None),
        P(rows, None, None),
        P("pair", rows, None, None, None),
        P("pair", rows, None, None),
        P("pair", rows, None, None),
    )

    def run(*args):
        local_heads = args[1].shape[1] // sizes["head"]
        body = functools.partial(on_device, swap=swap(local_heads, sizes, args[0].shape[2] // sizes["pair"], args[4].shape[3]))
        step = jax.shard_map(
            body, mesh=fine, in_specs=in_specs, out_specs=out_specs, check_vma=False
        )
        return step(*args)

    return run
```
